512 devices in a mesh: row: 32 (over z_lo, y), col: 16 (over x, z_hi, core).
Axes of the slice: x: 4, y: 8, z: 8 (z_hi: 2, z_lo: 4; z = z_hi * 4 + z_lo), core: 2. Of those that a mesh axis runs over, the one named last changes fastest.
Arguments:
- queries: bfloat16 [1, 32, 32, 64, 2048], P(None, 'row', 'col'), may hold values from -17 to 17
- keys: bfloat16 [1, 32, 32, 64, 2048], P(None, 'row', 'col'), may hold values from -5.5 to 5.5
- values: bfloat16 [1, 32, 32, 64, 2048], P(None, 'row', 'col'), may hold values from -6 to 6
- pool_keys: bfloat16 [1024, 16, 2048], P(('row', 'col')), may hold values from -6 to 6
- pool_values: bfloat16 [1024, 16, 2048], P(('row', 'col')), may hold values from -6 to 6
- top_keys: bfloat16 [1, 128, 2048], P(None, 'col'), may hold values from -6 to 6
- top_values: bfloat16 [1, 128, 2048], P(None, 'col'), may hold values from -6 to 6
- coarse_ids: int32 [1, 32, 32, 8], P(None, 'row', 'col'), may hold values from 0 to 1023, as said below
Outputs:
- attended: bfloat16 [1, 32, 32, 64, 2048], P(None, 'row', 'col')
The draws below stay inside these ranges and needn't reach their ends.
Inputs may be any that keep to these rules, and one draw needn't show every extreme that they name: Entry coarse_ids[n, i, j, c] names a pool block held by the device that holds fine block (i, j) or by one of its eight neighbours in the mesh (no wrap); the device with row index r and col index q holds pool blocks (r * 16 + q) * 2 to (r * 16 + q + 1) * 2 - 1. The 8 entries of a fine block differ.
All inputs are finite; a program needn't handle non-finite values.
Results may differ from the reference program's by a relative error of at most 0.0049.
Values may be sent and summed in bfloat16 or wider, within the bound.
No kernel may reach another device: no remote copies, remote signals or barrier semaphores. Data moves between devices by JAX's collectives and lax.ppermute only.
A program may use at most 64 MiB of HBM per device.

```python
import math
import jax
import jax.numpy as jnp
from jax import lax

D = 2048
HEADS = 16
BT = 64
CT = 16
CB = 2
NCB = 8
IMAGES = 1
BR = 1
BC = 2
NBR = 32
NBC = 32
POOL = 1024
TOP = 128


def query_key_pair(key):
    shape = (IMAGES, NBR, NBC, BT, D)
    query_seed = jax.random.fold_in(key, 11)
    key_seed = jax.random.fold_in(key, 12)
    keys_drawn = jnp.clip(jax.random.normal(key_seed, shape, jnp.float32), -4.0, 4.0)
    queries_drawn = 2.0 * jnp.clip(jax.random.normal(query_seed, shape, jnp.float32), -4.0, 4.0)
    return (queries_drawn, keys_drawn)


def draw_queries(key, part):
    return query_key_pair(key)[0].astype(jnp.bfloat16)


def draw_keys(key, part):
    return query_key_pair(key)[1].astype(jnp.bfloat16)


def draw_coarse_ids(key, part):
    slot_total = 9 * CB
    shape = (IMAGES, NBR, NBC, slot_total)
    mesh_rows = NBR // BR
    mesh_cols = NBC // BC
    slot_number = jnp.arange(slot_total, dtype=jnp.int32)
    offset_number = slot_number // CB
    row_shift = offset_number // 3 - 1
    col_shift = offset_number % 3 - 1
    local_number = slot_number % CB
    device_row = (jnp.arange(NBR, dtype=jnp.int32) // BR).reshape(1, NBR, 1, 1)
    device_col = (jnp.arange(NBC, dtype=jnp.int32) // BC).reshape(1, 1, NBC, 1)
    owner_row = device_row + row_shift
    owner_col = device_col + col_shift
    inside = (owner_row >= 0) & (owner_row < mesh_rows) & (owner_col >= 0) & (owner_col < mesh_cols)
    priority = jax.random.randint(jax.random.fold_in(key, 21), shape, 0, 2 ** 20, dtype=jnp.int32) * 64 + slot_number
    priority = jnp.where(inside, priority, priority - 2 ** 28)
    image_number = jnp.arange(IMAGES, dtype=jnp.int32).reshape(IMAGES, 1, 1, 1)
    block_row = jnp.arange(NBR, dtype=jnp.int32).reshape(1, NBR, 1, 1)
    block_col = jnp.arange(NBC, dtype=jnp.int32).reshape(1, 1, NBC, 1)
    first_pick = (image_number == 0) & (block_row == 0) & (block_col == 0) & (slot_number == 4 * CB)
    last_pick = (image_number == 0) & (block_row == NBR - 1) & (block_col == NBC - 1) & (slot_number == 5 * CB - 1)
    priority = priority + jnp.where(first_pick | last_pick, 2 ** 27, 0).astype(jnp.int32)
    chosen = lax.top_k(priority, NCB)[1]
    owner_device = owner_row * mesh_cols + owner_col
    full_ids = jnp.broadcast_to(owner_device * CB + local_number, shape).astype(jnp.int32)
    return jnp.take_along_axis(full_ids, chosen.astype(jnp.int32), axis=3).astype(jnp.int32)


def block_levels(key, extent, pieces, low, high):
    def one(axis_at, shards_of):
        steps = jax.random.uniform(jax.random.fold_in(jax.random.fold_in(key, 6), axis_at), (shards_of,), jnp.float32, low / len(pieces), high / len(pieces))
        return jnp.repeat(jnp.exp(steps), extent[axis_at] // shards_of).reshape((-1,) + (1,) * (len(extent) - axis_at - 1))

    gain = one(*pieces[0])
    for cut in pieces[1:]:
        gain = gain * one(*cut)
    return gain


def noise(stream_key, dims, deviation, bound, cuts=(), held_as=jnp.bfloat16):
    entries = deviation * jax.random.normal(stream_key, dims, jnp.float32)
    if cuts:
        entries = entries * block_levels(stream_key, dims, cuts, -0.22, 0.18)
    return jnp.clip(entries, -bound, bound).astype(held_as)


def setup_inputs(seed: int = 0) -> dict:
    key_list = jax.random.split(jax.random.key(seed), 9)
    queries = draw_queries(jax.random.fold_in(key_list[8], 71), 0)
    keys = draw_keys(jax.random.fold_in(key_list[8], 71), 0)
    values = noise(key_list[2], (IMAGES, NBR, NBC, BT, D), 1.0, 6.0, ((1, 32), (2, 16)))
    pool_keys = noise(key_list[3], (POOL, CT, D), 1.0, 6.0, ((0, 512),))
    pool_values = noise(key_list[4], (POOL, CT, D), 1.0, 6.0, ((0, 512),))
    top_keys = noise(key_list[5], (IMAGES, TOP, D), 1.0, 6.0, ((1, 16),))
    top_values = noise(key_list[6], (IMAGES, TOP, D), 1.0, 6.0, ((1, 16),))
    coarse_ids = draw_coarse_ids(jax.random.fold_in(key_list[8], 71), 0)
    return {"queries": queries, "keys": keys, "values": values, "pool_keys": pool_keys, "pool_values": pool_values, "top_keys": top_keys, "top_values": top_values, "coarse_ids": coarse_ids}


NEG_FILL = -1e+30

def reference(queries, keys, values, pool_keys, pool_values, top_keys, top_values, coarse_ids):
    head_width = D // HEADS
    score_scale = 1.0 / math.sqrt(head_width)
    padding = ((0, 0), (1, 1), (1, 1), (0, 0), (0, 0))
    padded_keys = jnp.pad(keys, padding)
    padded_values = jnp.pad(values, padding)
    column_number = jnp.arange(NBC, dtype=jnp.int32)

    def one_image(image_items):
        query_image, key_image, value_image, id_image, top_key_image, top_value_image = image_items
        top_key_heads = top_key_image.astype(jnp.float32).reshape(TOP, HEADS, head_width)
        top_value_heads = top_value_image.astype(jnp.float32).reshape(TOP, HEADS, head_width)

        def one_row(row_number):
            query_row = lax.dynamic_index_in_dim(query_image, row_number, 0, keepdims=False)
            query_row = query_row.astype(jnp.float32).reshape(NBC, BT, HEADS, head_width)
            key_rows = lax.dynamic_slice_in_dim(key_image, row_number, 3, 0)
            value_rows = lax.dynamic_slice_in_dim(value_image, row_number, 3, 0)
            id_row = lax.dynamic_index_in_dim(id_image, row_number, 0, keepdims=False)
            score_parts = []
            value_parts = []
            for row_step in range(3):
                row_valid = (row_number + row_step - 1 >= 0) & (row_number + row_step - 1 < NBR)
                for col_step in range(3):
                    col_valid = (column_number + col_step - 1 >= 0) & (column_number + col_step - 1 < NBC)
                    key_part = key_rows[row_step, col_step:col_step + NBC].astype(jnp.float32).reshape(NBC, BT, HEADS, head_width)
                    value_part = value_rows[row_step, col_step:col_step + NBC].astype(jnp.float32).reshape(NBC, BT, HEADS, head_width)
                    raw_scores = jnp.einsum('bqhd,bkhd->bhqk', query_row, key_part) * score_scale
                    valid_mask = (row_valid & col_valid).reshape(NBC, 1, 1, 1)
                    score_parts.append(jnp.where(valid_mask, raw_scores, NEG_FILL))
                    value_parts.append(value_part)
            coarse_keys = jnp.take(pool_keys, id_row, axis=0).astype(jnp.float32).reshape(NBC, NCB * CT, HEADS, head_width)
            coarse_values = jnp.take(pool_values, id_row, axis=0).astype(jnp.float32).reshape(NBC, NCB * CT, HEADS, head_width)
            score_parts.append(jnp.einsum('bqhd,bkhd->bhqk', query_row, coarse_keys) * score_scale)
            value_parts.append(coarse_values)
            score_parts.append(jnp.einsum('bqhd,khd->bhqk', query_row, top_key_heads) * score_scale)
            scores = jnp.concatenate(score_parts, axis=-1)
            row_peak = lax.optimization_barrier(jnp.max(scores, axis=-1, keepdims=True))
            exponent = jnp.exp(scores - row_peak)
            weights = lax.optimization_barrier((exponent / lax.optimization_barrier(jnp.sum(exponent, axis=-1, keepdims=True))).astype(jnp.bfloat16))
            weights = weights.astype(jnp.float32)
            result = jnp.zeros((NBC, BT, HEADS, head_width), jnp.float32)
            offset = 0
            for value_part in value_parts:
                length = value_part.shape[1]
                result = result + jnp.einsum('bhqk,bkhd->bqhd', weights[..., offset:offset + length], value_part)
                offset = offset + length
            result = result + jnp.einsum('bhqk,khd->bqhd', weights[..., offset:], top_value_heads)
            return result.reshape(NBC, BT, D).astype(jnp.bfloat16)
        return lax.map(one_row, jnp.arange(NBR, dtype=jnp.int32))
    return lax.map(one_image, (queries, padded_keys, padded_values, coarse_ids, top_keys, top_values))
```

```python
import math

import jax
import jax.numpy as jnp
from jax import lax
from jax.experimental import pallas as pl
from jax.experimental.pallas import tpu as pltpu
from jax.sharding import PartitionSpec as P

HEADS = 16
NEG_FILL = -1e30
AXES = ("row", "col")
LANES = 128


def pairs(rows, cols, target):
    out = []
    for row in range(rows):
        for col in range(cols):
            there = target(row, col)
            if 0 <= there[0] < rows and 0 <= there[1] < cols:
                out.append((row * cols + col, there[0] * cols + there[1]))
    return out


def send(block, links):
    return lax.ppermute(block, AXES, links)


def copy_all(copies):
    for copy in copies:
        copy.start()
    for copy in copies:
        copy.wait()


def pack_kernel(side, keys, values, pool_keys, pool_values, top_keys, top_values, near, far, top, sems):
    tokens = keys.shape[1]
    pool = pool_keys.shape[0]
    copies = []
    for out, block in ((far, side[0]), (near, 1 - side[0])):
        place = 0
        for source, count in (
            (keys.at[block], tokens),
            (pool_keys, pool),
            (values.at[block], tokens),
            (pool_values, pool),
        ):
            copies.append((source, out.at[pl.ds(place, count)]))
            place += count
    copies.append((top_keys, top.at[0]))
    copies.append((top_values, top.at[1]))
    copy_all([pltpu.make_async_copy(a, b, sems.at[i]) for i, (a, b) in enumerate(copies)])


def pack(side, keys, values, pool_keys, pool_values, top_keys, top_values):
    tokens, width = keys.shape[1:]
    pool = pool_keys.shape[0]
    message = jax.ShapeDtypeStruct((2 * (tokens + pool), width), keys.dtype)
    share = jax.ShapeDtypeStruct((2,) + top_keys.shape, keys.dtype)
    return pl.pallas_call(
        pack_kernel,
        out_shape=(message, message, share),
        in_specs=[pl.BlockSpec(memory_space=pltpu.SMEM)] + [pl.BlockSpec(memory_space=pl.ANY)] * 6,
        out_specs=[pl.BlockSpec(memory_space=pltpu.VMEM)] * 3,
        scratch_shapes=[pltpu.SemaphoreType.DMA((10,))],
        name="pack",
    )(side, keys, values, pool_keys, pool_values, top_keys, top_values)


def split_in_three(value):
    high = value.astype(jnp.bfloat16)
    rest = value - high.astype(jnp.float32)
    middle = rest.astype(jnp.bfloat16)
    low = (rest - middle.astype(jnp.float32)).astype(jnp.bfloat16)
    return high, middle, low


def attend_kernel(
    q_own, q_up, q_down, keys, values, pool_keys, pool_values, near, far, top_a, top_b, bias,
    out_own, out_up, out_down,
    qs, ks, vs, tks, tvs, sems,
):
    own = keys.shape[0]
    pool = pool_keys.shape[0]
    edge = near.shape[0] // 2
    half_top = top_a.shape[1]
    rows = q_own.shape[0]
    width = q_own.shape[1]
    used = own + edge + pool + edge
    total = ks.shape[0]
    group = rows // 2
    copies = []
    for i, ref in enumerate((q_own, q_up, q_down)):
        copies.append((ref, qs.at[pl.ds(i * rows, rows)]))
    for part, scratch, mine, mine_pool in ((0, ks, keys, pool_keys), (1, vs, values, pool_values)):
        place = 0
        for ref, count in (
            (mine, own),
            (near.at[pl.ds(part * edge, edge)], edge),
            (mine_pool, pool),
            (far.at[pl.ds(part * edge, edge)], edge),
        ):
            copies.append((ref, scratch.at[pl.ds(place, count)]))
            place += count
    for part, scratch in ((0, tks), (1, tvs)):
        copies.append((top_a.at[part], scratch.at[pl.ds(0, half_top)]))
        copies.append((top_b.at[part], scratch.at[pl.ds(half_top, half_top)]))
    started = [pltpu.make_async_copy(a, b, sems.at[i]) for i, (a, b) in enumerate(copies)]
    for copy in started:
        copy.start()
    ks[pl.ds(used, total - used), :] = jnp.zeros((total - used, width), ks.dtype)
    vs[pl.ds(used, total - used), :] = jnp.zeros((total - used, width), vs.dtype)
    for copy in started:
        copy.wait()
    scale = 1.0 / math.sqrt(width // HEADS)
    lane = lax.broadcasted_iota(jnp.int32, (rows, LANES), 1)
    logs = [jnp.zeros((rows, LANES), jnp.float32) for _ in range(3)]
    ones = jnp.ones((total, LANES), jnp.bfloat16)
    ones_top = jnp.ones((2 * half_top, LANES), jnp.bfloat16)
    nt = (((1,), (1,)), ((), ()))
    for head in range(HEADS):
        part = pl.ds(head * LANES, LANES)
        query = qs[:, part]
        scores = lax.dot_general(query, ks[:, part], nt, preferred_element_type=jnp.float32) * scale
        top_scores = (
            lax.dot_general(query[:rows], tks[:, part], nt, preferred_element_type=jnp.float32) * scale
        )
        weights = []
        peaks = []
        for i in range(6):
            piece = scores[i * group : (i + 1) * group] + bias[pl.ds(i, 1), :]
            peak = jnp.max(piece, axis=1, keepdims=True)
            if i < 2:
                peak = jnp.maximum(
                    peak, jnp.max(top_scores[i * group : (i + 1) * group], axis=1, keepdims=True)
                )
            peaks.append(peak)
            weights.append(jnp.exp(piece - peak).astype(jnp.bfloat16))
        value = jnp.concatenate([vs[:, part], ones], axis=1)
        summed = jnp.dot(
            jnp.concatenate(weights, axis=0), value, preferred_element_type=jnp.float32
        )
        top_weights = jnp.exp(top_scores - jnp.concatenate(peaks[:2], axis=0)).astype(jnp.bfloat16)
        top_value = jnp.concatenate([tvs[:, part], ones_top], axis=1)
        top_summed = jnp.dot(top_weights, top_value, preferred_element_type=jnp.float32)
        for i, out in enumerate((out_own, out_up, out_down)):
            piece = summed[i * rows : (i + 1) * rows]
            if i == 0:
                piece = piece + top_summed
            norm = piece[:, LANES:]
            out[:, part] = (piece[:, :LANES] / norm).astype(out.dtype)
            log = jnp.concatenate(peaks[2 * i : 2 * i + 2], axis=0) + jnp.log(norm)
            logs[i] = jnp.where(lane == head, log, logs[i])
    tail = pl.ds(width, LANES)
    out_own[:, tail] = logs[0]
    for log, out in ((logs[1], out_up), (logs[2], out_down)):
        high, middle, low = (x.astype(jnp.float32) for x in split_in_three(log))
        out[:, tail] = (
            high + pltpu.roll(middle, HEADS, 1) + pltpu.roll(low, 2 * HEADS, 1)
        ).astype(out.dtype)


def attend(q_own, q_up, q_down, keys, values, pool_keys, pool_values, near, far, top_a, top_b, bias):
    rows, width = q_own.shape
    total = bias.shape[1]
    top = 2 * top_a.shape[1]
    message = (rows, width + LANES)
    bf16 = jnp.bfloat16
    return pl.pallas_call(
        attend_kernel,
        out_shape=(
            jax.ShapeDtypeStruct(message, jnp.float32),
            jax.ShapeDtypeStruct(message, bf16),
            jax.ShapeDtypeStruct(message, bf16),
        ),
        in_specs=[pl.BlockSpec(memory_space=pl.ANY)] * 11 + [pl.BlockSpec(memory_space=pltpu.VMEM)],
        out_specs=[pl.BlockSpec(memory_space=pltpu.VMEM)] * 3,
        scratch_shapes=[
            pltpu.VMEM((3 * rows, width), bf16),
            pltpu.VMEM((total, width), bf16),
            pltpu.VMEM((total, width), bf16),
            pltpu.VMEM((top, width), bf16),
            pltpu.VMEM((top, width), bf16),
            pltpu.SemaphoreType.DMA((15,)),
        ],
        cost_estimate=pl.CostEstimate(
            flops=4 * 3 * rows * total * width, bytes_accessed=8 << 20, transcendentals=3 * rows * total * HEADS
        ),
        name="attend",
    )(q_own, q_up, q_down, keys, values, pool_keys, pool_values, near, far, top_a, top_b, bias)


def merge_kernel(edges, own, above, below, out):
    rows, width = out.shape
    tail = pl.ds(width, LANES)
    logs = [own[:, tail]]
    for i, ref in enumerate((above, below)):
        coded = ref[:, tail].astype(jnp.float32)
        log = coded + pltpu.roll(coded, LANES - HEADS, 1) + pltpu.roll(coded, LANES - 2 * HEADS, 1)
        logs.append(jnp.where(edges[i] > 0, log, NEG_FILL))
    peak = jnp.maximum(jnp.maximum(logs[0], logs[1]), logs[2])
    shares = [jnp.exp(log - peak) for log in logs]
    norm = shares[0] + shares[1] + shares[2]
    shares = [share / norm for share in shares]
    for head in range(HEADS):
        part = pl.ds(head * LANES, LANES)
        result = own[:, part] * shares[0][:, head : head + 1]
        result = result + above[:, part].astype(jnp.float32) * shares[1][:, head : head + 1]
        result = result + below[:, part].astype(jnp.float32) * shares[2][:, head : head + 1]
        out[:, part] = result.astype(out.dtype)


def merge(edges, own, above, below, width):
    return pl.pallas_call(
        merge_kernel,
        out_shape=jax.ShapeDtypeStruct((own.shape[0], width), jnp.bfloat16),
        in_specs=[pl.BlockSpec(memory_space=pltpu.SMEM)] + [pl.BlockSpec(memory_space=pltpu.VMEM)] * 3,
        out_specs=pl.BlockSpec(memory_space=pltpu.VMEM),
        name="merge",
    )(edges, own, above, below)


def body(queries, keys, values, pool_keys, pool_values, top_keys, top_values, coarse_ids):
    _, _, blocks, tokens, width = queries.shape
    pool_blocks, pool_tokens, _ = pool_keys.shape
    rows = lax.axis_size("row")
    cols = lax.axis_size("col")
    row = lax.axis_index("row")
    col = lax.axis_index("col")
    side = col % 2
    pool = pool_blocks * pool_tokens
    own = blocks * tokens

    up = pairs(rows, cols, lambda r, q: (r - 1, q))
    down = pairs(rows, cols, lambda r, q: (r + 1, q))
    partner = pairs(rows, cols, lambda r, q: (r, q ^ 1))
    across = pairs(rows, cols, lambda r, q: (r, q + 1 if q % 2 else q - 1))
    line = rows // 4
    halves = pairs(rows, cols, lambda r, q: ((3 - r // line) * line + r % line, q ^ 2))
    step_one = pairs(rows, cols, lambda r, q: (r, q ^ 4))
    step_two = pairs(rows, cols, lambda r, q: (r, q ^ 8))

    query = queries.reshape(own, width)
    pk = pool_keys.reshape(pool, width)
    pv = pool_values.reshape(pool, width)
    near, far, top = pack(
        side.reshape(1),
        keys.reshape(blocks, tokens, width),
        values.reshape(blocks, tokens, width),
        pk,
        pv,
        top_keys[0],
        top_values[0],
    )
    far = send(far, across)
    q_up = send(query, down)
    q_down = send(query, up)
    near = send(near, partner)
    for links in (halves, step_one, step_two):
        top = jnp.concatenate([top, send(top, links)], axis=1)
    top_other = send(top, partner)
    ids = coarse_ids.reshape(blocks, -1)
    ids_up = send(ids, down)
    ids_down = send(ids, up)

    other = col + 1 - 2 * side
    beyond = col - 1 + 2 * side
    exists = (beyond >= 0) & (beyond < cols)
    group_block = jnp.tile(jnp.arange(blocks, dtype=jnp.int32), 3)
    all_ids = jnp.concatenate([ids, ids_up, ids_down], axis=0)

    def pool_bias(holder):
        first = (row * cols + holder) * pool_blocks
        block = first + jnp.arange(pool, dtype=jnp.int32) // pool_tokens
        return (all_ids[:, :, None] == block[None, None, :]).any(axis=1)

    def fine(valid):
        return jnp.broadcast_to(valid[:, None], (3 * blocks, tokens))

    full = jnp.ones((3 * blocks, own), bool)
    valid = jnp.concatenate(
        [
            full,
            fine(group_block == 1 - side),
            pool_bias(other),
            pool_bias(col),
            fine((group_block == side) & exists),
            pool_bias(beyond) & exists,
        ],
        axis=1,
    )
    gap = -valid.shape[1] % LANES
    valid = jnp.pad(valid, ((0, 0), (0, gap)))
    bias = jnp.where(valid, 0.0, NEG_FILL).astype(jnp.float32)

    mine, to_up, to_down = attend(
        query, q_up, q_down, keys.reshape(own, width), values.reshape(own, width), pk, pv,
        near, far, top, top_other, bias,
    )
    below = send(to_up, up)
    above = send(to_down, down)
    edges = jnp.stack([row > 0, row < rows - 1]).astype(jnp.int32)
    return merge(edges, mine, above, below, width).reshape(queries.shape)


def solution(mesh):
    placed = (
        P(None, "row", "col", None, None),
        P(None, "row", "col", None, None),
        P(None, "row", "col", None, None),
        P(("row", "col"), None, None),
        P(("row", "col"), None, None),
        P(None, "col", None),
        P(None, "col", None),
        P(None, "row", "col", None),
    )
    return jax.shard_map(
        body,
        mesh=mesh,
        in_specs=placed,
        out_specs=P(None, "row", "col", None, None),
        check_vma=False,
    )
```

```python
import math

import jax
import jax.numpy as jnp
from jax import lax
from jax.experimental import pallas as pl
from jax.experimental.pallas import tpu as pltpu
from jax.sharding import PartitionSpec as P


HEADS = 16
NEG_FILL = -1e30
AXES = ("row", "col")
LANES = 128


def pairs(rows, cols, target):
    out = []
    for row in range(rows):
        for col in range(cols):
            there = target(row, col)
            if 0 <= there[0] < rows and 0 <= there[1] < cols:
                out.append((row * cols + col, there[0] * cols + there[1]))
    return out


def send(block, links):
    return lax.ppermute(block, AXES, links)


def pack_kernel(side, query, keys, values, pool_keys, pool_values, top_keys, top_values, near, far, top, first, second, sems):
    tokens = keys.shape[1]
    pool = pool_keys.shape[0]
    copies = []
    for out, block in ((far, side[0]), (near, 1 - side[0])):
        place = 0
        for source, count in (
            (keys.at[block], tokens),
            (pool_keys, pool),
            (values.at[block], tokens),
            (pool_values, pool),
        ):
            copies.append((source, out.at[pl.ds(place, count)]))
            place += count
    copies.append((top_keys, top.at[0]))
    copies.append((top_values, top.at[1]))
    copies.append((query.at[0], first))
    copies.append((query.at[1], second))
    run([pltpu.make_async_copy(a, b, sems.at[i]) for i, (a, b) in enumerate(copies)])


def pack(side, query, keys, values, pool_keys, pool_values, top_keys, top_values):
    tokens, width = keys.shape[1:]
    pool = pool_keys.shape[0]
    message = jax.ShapeDtypeStruct((2 * (tokens + pool), width), keys.dtype)
    share = jax.ShapeDtypeStruct((2,) + top_keys.shape, keys.dtype)
    block = jax.ShapeDtypeStruct((tokens, width), keys.dtype)
    return pl.pallas_call(
        pack_kernel,
        out_shape=(message, message, share, block, block),
        in_specs=[pl.BlockSpec(memory_space=pltpu.SMEM)] + [pl.BlockSpec(memory_space=pltpu.HBM)] * 7,
        out_specs=[pl.BlockSpec(memory_space=pltpu.VMEM)] * 5,
        scratch_shapes=[pltpu.SemaphoreType.DMA((12,))],
        compiler_params=pltpu.CompilerParams(vmem_limit_bytes=6 << 20),
        name="pack",
    )(side, query, keys, values, pool_keys, pool_values, top_keys, top_values)


def split_in_three(value):
    high = value.astype(jnp.bfloat16)
    rest = value - high.astype(jnp.float32)
    middle = rest.astype(jnp.bfloat16)
    low = (rest - middle.astype(jnp.float32)).astype(jnp.bfloat16)
    return high, middle, low


NT = (((1,), (1,)), ((), ()))


def fill(scratch, spans, sems, first):
    copies = []
    place = 0
    for ref in spans:
        count = ref.shape[0]
        copies.append(pltpu.make_async_copy(ref, scratch.at[pl.ds(place, count)], sems.at[first + len(copies)]))
        place += count
    return copies


def halves_of(ref):
    edge = ref.shape[0] // 2
    return ref.at[pl.ds(0, edge)], ref.at[pl.ds(edge, edge)]


def run(copies):
    for copy in copies:
        copy.start()
    for copy in copies:
        copy.wait()


def weigh(scores, bias, group, before=None):
    peaks, weights = [], []
    for i in range(scores.shape[0] // group):
        piece = scores[i * group : (i + 1) * group] + bias[pl.ds(i, 1), :]
        peak = jnp.max(piece, axis=1, keepdims=True)
        if before is not None:
            peak = jnp.maximum(before[i], peak)
        peaks.append(peak)
        weights.append(jnp.exp(piece - peak).astype(jnp.bfloat16))
    return peaks, jnp.concatenate(weights, axis=0)


def near_kernel(
    ends, q_up, q_down, bound, passed, keys, values, pool_keys, pool_values, near, bias,
    qs, sums, tops, norms, ks, vs, sems,
):
    rows, width = q_up.shape
    group = rows // 2
    near_keys, near_values = halves_of(near)
    copies = (
        fill(qs, (*halves_of(q_up), *halves_of(q_down)), sems, 0)
        + fill(ks, (keys, near_keys, pool_keys), sems, 4)
        + fill(vs, (values, near_values, pool_values), sems, 7)
    )
    for i in range(2):
        apart = fill(qs.at[pl.ds(i * rows, rows)], (bound, passed), sems, 2 * i)

        @pl.when(ends[i] > 0)
        def _():
            for copy in apart:
                copy.start()

        @pl.when(ends[i] == 0)
        def _():
            for copy in copies[2 * i : 2 * i + 2]:
                copy.start()

    for copy in copies[4:]:
        copy.start()
    for copy in copies:
        copy.wait()
    scale = 1.0 / math.sqrt(width // HEADS)
    ones = jnp.ones((ks.shape[0], LANES), jnp.bfloat16)
    for head in range(HEADS):
        part = pl.ds(head * LANES, LANES)
        scores = lax.dot_general(qs[:, part], ks[:, part], NT, preferred_element_type=jnp.float32) * scale
        peaks, weights = weigh(scores, bias, group)
        value = jnp.concatenate([vs[:, part], ones], axis=1)
        summed = jnp.dot(weights, value, preferred_element_type=jnp.float32)
        sums[:, part] = summed[:, :LANES]
        norms[:, part] = summed[:, LANES:]
        for i, peak in enumerate(peaks):
            tops[pl.ds(i * group, group), part] = jnp.broadcast_to(peak, (group, LANES))


def near_attention(ends, q_up, q_down, bound, passed, keys, values, pool_keys, pool_values, near, bias):
    rows, width = q_up.shape
    total = bias.shape[1]
    bf16, f32 = jnp.bfloat16, jnp.float32
    held, sent = pltpu.HBM, pl.ANY
    places = (pltpu.SMEM, sent, sent, sent, sent, held, held, held, held, sent, pltpu.VMEM)
    return pl.pallas_call(
        near_kernel,
        out_shape=[jax.ShapeDtypeStruct((2 * rows, width), kind) for kind in (bf16, f32, f32, f32)],
        in_specs=[pl.BlockSpec(memory_space=place) for place in places],
        out_specs=[pl.BlockSpec(memory_space=pltpu.VMEM)] * 4,
        scratch_shapes=[
            pltpu.VMEM((total, width), bf16),
            pltpu.VMEM((total, width), bf16),
            pltpu.SemaphoreType.DMA((10,)),
        ],
        compiler_params=pltpu.CompilerParams(vmem_limit_bytes=16 << 20),
        cost_estimate=pl.CostEstimate(
            flops=4 * 2 * rows * total * width, bytes_accessed=4 << 20, transcendentals=2 * rows * total * HEADS
        ),
        name="near_attention",
    )(ends, q_up, q_down, bound, passed, keys, values, pool_keys, pool_values, near, bias)


def far_kernel(qs, sums, tops, norms, far, bias, out_up, out_down, ks, vs):
    edge = far.shape[0] // 2
    rows = out_up.shape[0]
    width = qs.shape[1]
    group = rows // 2
    scale = 1.0 / math.sqrt(width // HEADS)
    for part, scratch in ((0, ks), (1, vs)):
        scratch[pl.ds(0, edge), :] = far[pl.ds(part * edge, edge), :]
        scratch[pl.ds(edge, LANES - edge), :] = jnp.zeros((LANES - edge, width), scratch.dtype)
    lane = lax.broadcasted_iota(jnp.int32, (group, LANES), 1)
    zero = jnp.zeros((group, LANES), jnp.float32)
    kept_peak, kept_norm = [zero] * 4, [zero + 1.0] * 4
    ones = jnp.ones((LANES, LANES), jnp.bfloat16)
    outs = (out_up, out_down)
    spans = [pl.ds(i * group, group) for i in range(4)]
    for head in range(HEADS):
        part = pl.ds(head * LANES, LANES)
        scores = lax.dot_general(qs[:, part], ks[:, part], NT, preferred_element_type=jnp.float32) * scale
        before = [tops[span, part] for span in spans]
        peaks, weights = weigh(scores, bias, group, before)
        value = jnp.concatenate([vs[:, part], ones], axis=1)
        summed = jnp.dot(weights, value, preferred_element_type=jnp.float32)
        for i, span in enumerate(spans):
            factor = jnp.exp(before[i] - peaks[i])
            piece = summed[i * group : (i + 1) * group]
            norm = norms[span, part] * factor + piece[:, LANES:]
            result = (sums[span, part] * factor + piece[:, :LANES]) / norm
            outs[i // 2][spans[i % 2], part] = result.astype(jnp.bfloat16)
            kept_peak[i] = jnp.where(lane == head, peaks[i], kept_peak[i])
            kept_norm[i] = jnp.where(lane == head, norm, kept_norm[i])
    for i in range(4):
        high, middle, low = split_in_three(kept_peak[i] + jnp.log(kept_norm[i]))
        middle = pltpu.roll(middle.astype(jnp.float32), HEADS, 1)
        low = pltpu.roll(low.astype(jnp.float32), 2 * HEADS, 1)
        outs[i // 2][spans[i % 2], pl.ds(width, LANES)] = (high.astype(jnp.float32) + middle + low).astype(jnp.bfloat16)


def far_attention(qs, sums, tops, norms, far, bias):
    rows, width = qs.shape[0] // 2, qs.shape[1]
    message = jax.ShapeDtypeStruct((rows, width + LANES), jnp.bfloat16)
    return pl.pallas_call(
        far_kernel,
        out_shape=(message, message),
        in_specs=[pl.BlockSpec(memory_space=pltpu.VMEM)] * 6,
        out_specs=[pl.BlockSpec(memory_space=pltpu.VMEM)] * 2,
        scratch_shapes=[pltpu.VMEM((LANES, width), jnp.bfloat16)] * 2,
        compiler_params=pltpu.CompilerParams(vmem_limit_bytes=16 << 20),
        cost_estimate=pl.CostEstimate(
            flops=4 * 2 * rows * LANES * width, bytes_accessed=4 << 20, transcendentals=2 * rows * LANES * HEADS
        ),
        name="far_attention",
    )(qs, sums, tops, norms, far, bias)


def own_kernel(query, keys, values, pool_keys, pool_values, near, far, top_a, top_b, bias, out, logs, qs, ks, vs, sems):
    rows, width = query.shape
    group = rows // 2
    gap = ks.shape[0] - keys.shape[0] - near.shape[0] // 2 - pool_keys.shape[0] - far.shape[0] // 2 - 2 * top_a.shape[1]
    copies = [pltpu.make_async_copy(query, qs, sems.at[0])]
    for part, scratch, mine, pool in ((0, ks, keys, pool_keys), (1, vs, values, pool_values)):
        spans = (top_a.at[part], top_b.at[part], mine, halves_of(near)[part], pool, halves_of(far)[part])
        copies += fill(scratch, spans, sems, 1 + 6 * part)
    for copy in copies:
        copy.start()
    for scratch in (ks, vs):
        scratch[pl.ds(ks.shape[0] - gap, gap), :] = jnp.zeros((gap, width), scratch.dtype)
    for copy in copies:
        copy.wait()
    scale = 1.0 / math.sqrt(width // HEADS)
    ones = jnp.ones((ks.shape[0], LANES), jnp.bfloat16)
    for head in range(HEADS):
        part = pl.ds(head * LANES, LANES)
        scores = lax.dot_general(qs[:, part], ks[:, part], NT, preferred_element_type=jnp.float32) * scale
        peaks, weights = weigh(scores, bias, group)
        value = jnp.concatenate([vs[:, part], ones], axis=1)
        summed = jnp.dot(weights, value, preferred_element_type=jnp.float32)
        norm = summed[:, LANES:]
        out[:, part] = summed[:, :LANES] / norm
        for i, peak in enumerate(peaks):
            span = pl.ds(i * group, group)
            logs[span, part] = peak + jnp.log(norm[i * group : (i + 1) * group])


def own_attention(query, keys, values, pool_keys, pool_values, near, far, top_a, top_b, bias):
    rows, width = query.shape
    total = bias.shape[1]
    bf16, f32 = jnp.bfloat16, jnp.float32
    held, sent = pltpu.HBM, pl.ANY
    places = (held, held, held, held, held, sent, sent, sent, sent, pltpu.VMEM)
    return pl.pallas_call(
        own_kernel,
        out_shape=[jax.ShapeDtypeStruct((rows, width), f32)] * 2,
        in_specs=[pl.BlockSpec(memory_space=place) for place in places],
        out_specs=[pl.BlockSpec(memory_space=pltpu.VMEM)] * 2,
        scratch_shapes=[
            pltpu.VMEM((rows, width), bf16),
            pltpu.VMEM((total, width), bf16),
            pltpu.VMEM((total, width), bf16),
            pltpu.SemaphoreType.DMA((13,)),
        ],
        compiler_params=pltpu.CompilerParams(vmem_limit_bytes=16 << 20),
        cost_estimate=pl.CostEstimate(
            flops=4 * rows * total * width, bytes_accessed=4 << 20, transcendentals=rows * total * HEADS
        ),
        name="own_attention",
    )(query, keys, values, pool_keys, pool_values, near, far, top_a, top_b, bias)


def merge_kernel(edges, own, own_logs, above, below, out):
    _, width = out.shape
    tail = pl.ds(width, LANES)
    logs = []
    for i, ref in enumerate((above, below)):
        coded = ref[:, tail].astype(jnp.float32)
        log = coded + pltpu.roll(coded, LANES - HEADS, 1) + pltpu.roll(coded, LANES - 2 * HEADS, 1)
        logs.append(jnp.where(edges[i] > 0, log, NEG_FILL))
    for head in range(HEADS):
        part = pl.ds(head * LANES, LANES)
        own_log = own_logs[:, part]
        up_log, down_log = (jnp.broadcast_to(log[:, head : head + 1], own_log.shape) for log in logs)
        peak = jnp.maximum(jnp.maximum(own_log, up_log), down_log)
        shares = [jnp.exp(log - peak) for log in (own_log, up_log, down_log)]
        result = own[:, part] * shares[0]
        result = result + above[:, part].astype(jnp.float32) * shares[1]
        result = result + below[:, part].astype(jnp.float32) * shares[2]
        out[:, part] = (result / (shares[0] + shares[1] + shares[2])).astype(out.dtype)


def merge(edges, own, own_logs, above, below):
    return pl.pallas_call(
        merge_kernel,
        out_shape=jax.ShapeDtypeStruct(own.shape, jnp.bfloat16),
        in_specs=[pl.BlockSpec(memory_space=pltpu.SMEM)] + [pl.BlockSpec(memory_space=pltpu.VMEM)] * 4,
        out_specs=pl.BlockSpec(memory_space=pltpu.VMEM),
        compiler_params=pltpu.CompilerParams(vmem_limit_bytes=8 << 20),
        name="merge",
    )(edges, own, own_logs, above, below)


def body(queries, keys, values, pool_keys, pool_values, top_keys, top_values, coarse_ids):
    _, _, blocks, tokens, width = queries.shape
    pool_blocks, pool_tokens, _ = pool_keys.shape
    rows = lax.axis_size("row")
    cols = lax.axis_size("col")
    row = lax.axis_index("row")
    col = lax.axis_index("col")
    side = col % 2
    pool = pool_blocks * pool_tokens
    own = blocks * tokens

    up = pairs(rows, cols, lambda r, q: (r - 1, q))
    down = pairs(rows, cols, lambda r, q: (r + 1, q))
    partner = pairs(rows, cols, lambda r, q: (r, q ^ 1))
    across = pairs(rows, cols, lambda r, q: (r, q + 1 if q % 2 else q - 1))
    line = rows // 4
    nowhere = (-1, -1)
    at_start = lambda r: r % line == 0
    at_end = lambda r: r % line == line - 1
    up_inside = pairs(rows, cols, lambda r, q: nowhere if at_start(r) else (r - 1, q))
    down_inside = pairs(rows, cols, lambda r, q: nowhere if at_end(r) else (r + 1, q))
    between = pairs(rows, cols, lambda r, q: (r + 1, q) if at_end(r) else (r - 1, q) if at_start(r) else nowhere)
    along_z = pairs(rows, cols, lambda r, q: (r + line, q) if at_end(r) else (r - line, q) if at_start(r) else nowhere)
    round_y = pairs(
        rows,
        cols,
        lambda r, q: (r - line + 1, q)
        if at_end(r) and r >= line
        else (r + line - 1, q)
        if at_start(r) and r < rows - line
        else nowhere,
    )
    halves = pairs(rows, cols, lambda r, q: ((3 - r // line) * line + r % line, q ^ 2))
    step_one = pairs(rows, cols, lambda r, q: (r, q ^ 4))
    step_two = pairs(rows, cols, lambda r, q: (r, q ^ 8))

    def stay(array, *shape):
        return pltpu.with_memory_space_constraint(array.reshape(shape), pltpu.HBM)

    query = queries.reshape(own, width)
    pk = stay(pool_keys, pool, width)
    pv = stay(pool_values, pool, width)
    near, far, top, first, second = pack(
        side.reshape(1),
        stay(queries, blocks, tokens, width),
        stay(keys, blocks, tokens, width),
        stay(values, blocks, tokens, width),
        pk,
        pv,
        stay(top_keys, *top_keys.shape[1:]),
        stay(top_values, *top_values.shape[1:]),
    )
    far = send(far, across)
    q_up = send(query, down_inside)
    q_down = send(query, up_inside)
    bound = send(first, between)
    passed = send(send(second, along_z), round_y)
    ends = jnp.stack([at_start(row), at_end(row)]).astype(jnp.int32)
    near = send(near, partner)
    for links in (step_one, step_two, halves):
        top = jnp.concatenate([top, send(top, links)], axis=1)
    top_other = send(top, partner)
    ids = coarse_ids.reshape(blocks, -1)
    ids_up = send(ids, down)
    ids_down = send(ids, up)

    other = col + 1 - 2 * side
    beyond = col - 1 + 2 * side
    exists = (beyond >= 0) & (beyond < cols)
    block_of = jnp.arange(blocks, dtype=jnp.int32)

    def bias_of(listed, count):
        def pool_valid(holder):
            first = (row * cols + holder) * pool_blocks
            block = first + jnp.arange(pool, dtype=jnp.int32) // pool_tokens
            return (listed[:, :, None] == block[None, None, :]).any(axis=1)

        def fine(valid):
            return jnp.broadcast_to(jnp.tile(valid, count)[:, None], (count * blocks, tokens))

        near_parts = [jnp.ones((count * blocks, own), bool), fine(block_of == 1 - side), pool_valid(other), pool_valid(col)]
        far_parts = [fine((block_of == side) & exists), pool_valid(beyond) & exists]
        far_parts.append(jnp.zeros((count * blocks, -(tokens + pool) % LANES), bool))
        as_bias = lambda parts: jnp.where(jnp.concatenate(parts, axis=1), 0.0, NEG_FILL).astype(jnp.float32)
        return as_bias(near_parts), as_bias(far_parts)

    near_bias, far_bias = bias_of(jnp.concatenate([ids_up, ids_down], axis=0), 2)
    own_bias = jnp.concatenate([jnp.zeros((blocks, 2 * top_other.shape[1]), jnp.float32), *bias_of(ids, 1)], axis=1)

    kept_keys, kept_values = stay(keys, own, width), stay(values, own, width)
    near_parts = near_attention(ends, q_up, q_down, bound, passed, kept_keys, kept_values, pk, pv, near, near_bias)
    to_up, to_down = far_attention(*near_parts, far, far_bias)
    below = send(to_up, up)
    above = send(to_down, down)
    mine = own_attention(
        stay(queries, own, width), kept_keys, kept_values, pk, pv, near, far, top, top_other, own_bias
    )
    edges = jnp.stack([row > 0, row < rows - 1]).astype(jnp.int32)
    return merge(edges, *mine, above, below).reshape(queries.shape)


def solution(mesh):
    placed = (
        P(None, "row", "col", None, None),
        P(None, "row", "col", None, None),
        P(None, "row", "col", None, None),
        P(("row", "col"), None, None),
        P(("row", "col"), None, None),
        P(None, "col", None),
        P(None, "col", None),
        P(None, "row", "col", None),
    )

    return jax.shard_map(
        body,
        mesh=mesh,
        in_specs=placed,
        out_specs=P(None, "row", "col", None, None),
        check_vma=False,
    )
```

```python
import functools
import math

import jax
import jax.numpy as jnp
from jax import lax
from jax.experimental import pallas as pl
from jax.experimental.pallas import tpu as pltpu
from jax.sharding import PartitionSpec as P


HEADS = 16
NEG_FILL = -1e30
AXES = ("row", "col")
LANES = 128
TILE = 8
BASE = 256


def pairs(rows, cols, target):
    out = []
    for row in range(rows):
        for col in range(cols):
            there = target(row, col)
            if 0 <= there[0] < rows and 0 <= there[1] < cols:
                out.append((row * cols + col, there[0] * cols + there[1]))
    return out


def send(block, links):
    return lax.ppermute(block, AXES, links)


def into(out, sources):
    copies, place = [], 0
    for ref in sources:
        copies.append((ref, out.at[pl.ds(place, ref.shape[0])]))
        place += ref.shape[0]
    return copies


def carry_out(copies, sems):
    run([pltpu.make_async_copy(a, b, sems.at[i]) for i, (a, b) in enumerate(copies)])


def pack_far_kernel(position, query, keys, values, pool_keys, pool_values, far, second, sems):
    block = lax.rem(position[1], 2)
    copies = into(far, (keys.at[block], pool_keys, values.at[block], pool_values))
    carry_out(copies + [(query.at[1], second)], sems)


def pack_near_kernel(
    position, ids, query, keys, values, pool_keys, pool_values, top_keys, top_values, near, top, message, bound, sems
):
    block = 1 - lax.rem(position[1], 2)
    blocks, _, _ = query.shape
    copies = into(near, (keys.at[block], pool_keys, values.at[block], pool_values))
    copies += [(top_keys, top.at[0]), (top_values, top.at[1])]
    copies += into(message, [query.at[i] for i in range(blocks)])
    copies += into(bound, [query.at[0]])
    started = [pltpu.make_async_copy(a, b, sems.at[i]) for i, (a, b) in enumerate(copies)]
    for copy in started:
        copy.start()
    count = ids.shape[1]
    line = lax.broadcasted_iota(jnp.int32, (TILE, LANES), 0)
    lane = lax.broadcasted_iota(jnp.int32, (TILE, LANES), 1)
    digits = jnp.zeros((TILE, LANES), jnp.int32)
    for i in range(blocks):
        for j in range(count):
            number = ids[i, j]
            digits = jnp.where((line == i) & (lane == j), number // BASE, digits)
            digits = jnp.where((line == i) & (lane == count + j), number % BASE, digits)
    digits = digits.astype(jnp.float32).astype(message.dtype)
    for out in (message, bound):
        tail = pl.ds(out.shape[0] - TILE, TILE)
        out[tail, :] = jnp.zeros((TILE, out.shape[1]), out.dtype)
        out[tail, pl.ds(0, LANES)] = digits
    for copy in started:
        copy.wait()


def join_kernel(first, second, out, sems):
    size = first.shape[1]
    pieces = []
    for i in range(2):
        pieces.append((first.at[i], out.at[i, pl.ds(0, size)]))
        pieces.append((second.at[i], out.at[i, pl.ds(size, size)]))
    carry_out(pieces, sems)


def join(first, second):
    shape = (2, 2 * first.shape[1], first.shape[2])
    return pl.pallas_call(
        join_kernel,
        out_shape=jax.ShapeDtypeStruct(shape, first.dtype),
        in_specs=[pl.BlockSpec(memory_space=pl.ANY)] * 2,
        out_specs=pl.BlockSpec(memory_space=pltpu.VMEM),
        scratch_shapes=[pltpu.SemaphoreType.DMA((4,))],
        compiler_params=pltpu.CompilerParams(vmem_limit_bytes=1 << 20),
        name="join",
    )(first, second)


def packed(kernel, outs, scalars, arrays, copies):
    dtype = arrays[0].dtype
    places = [pltpu.SMEM] * len(scalars) + [pltpu.HBM] * len(arrays)
    return pl.pallas_call(
        kernel,
        out_shape=[jax.ShapeDtypeStruct(shape, dtype) for shape in outs],
        in_specs=[pl.BlockSpec(memory_space=place) for place in places],
        out_specs=[pl.BlockSpec(memory_space=pltpu.VMEM)] * len(outs),
        scratch_shapes=[pltpu.SemaphoreType.DMA((copies,))],
        compiler_params=pltpu.CompilerParams(vmem_limit_bytes=4 << 20),
    )(*scalars, *arrays)


def split_in_three(value):
    high = value.astype(jnp.bfloat16)
    rest = value - high.astype(jnp.float32)
    middle = rest.astype(jnp.bfloat16)
    low = (rest - middle.astype(jnp.float32)).astype(jnp.bfloat16)
    return high, middle, low


NT = (((1,), (1,)), ((), ()))


def fill(scratch, spans, sems, first):
    copies = []
    place = 0
    for ref in spans:
        count = ref.shape[0]
        copies.append(pltpu.make_async_copy(ref, scratch.at[pl.ds(place, count)], sems.at[first + len(copies)]))
        place += count
    return copies


def halves_of(ref):
    edge = ref.shape[0] // 2
    return ref.at[pl.ds(0, edge)], ref.at[pl.ds(edge, edge)]


def run(copies):
    for copy in copies:
        copy.start()
    for copy in copies:
        copy.wait()


class Spot:
    def __init__(self, position, cols, blocks):
        row, col = position[0], position[1]
        self.side = lax.rem(col, 2)
        other = col + 1 - 2 * self.side
        beyond = col - 1 + 2 * self.side
        self.exists = jnp.where((beyond >= 0) & (beyond < cols), 1, 0)
        self.own, self.other, self.beyond = ((row * cols + holder) * blocks for holder in (col, other, beyond))
        self.blocks = blocks


def numbers_of(digits, count):
    digits = digits.astype(jnp.float32)
    lane = lax.broadcasted_iota(jnp.int32, digits.shape, 1)
    number = digits * BASE + pltpu.roll(digits, LANES - count, 1)
    return jnp.where(lane < count, number, -1.0).astype(jnp.int32)


def bias_of(numbers, spot, width, near, tokens, pool):
    lane = lax.broadcasted_iota(jnp.int32, (TILE, width), 1)
    line = lax.broadcasted_iota(jnp.int32, (TILE, width), 0)
    if near:
        start = 2 * tokens
        mine = jnp.where(line == 1 - spot.side, 1, 0)
        listed = jnp.where(lane < start, 1, 0)
        holders = (spot.other, spot.own)
    else:
        start = 0
        mine = jnp.where(line == spot.side, spot.exists, 0)
        listed = jnp.zeros((TILE, width), jnp.int32)
        holders = (spot.beyond,)
    listed = jnp.where((lane >= start) & (lane < start + tokens), mine, listed)
    start += tokens
    size = pool // spot.blocks
    for holder in holders:
        for i in range(spot.blocks):
            hit = jnp.max(jnp.where(numbers == holder + i, 1.0, 0.0), axis=1, keepdims=True)
            hit = jnp.broadcast_to(hit, (TILE, width)).astype(jnp.int32)
            if not near:
                hit = hit * spot.exists
            listed = jnp.where((lane >= start) & (lane < start + size), hit, listed)
            start += size
    return jnp.where(listed > 0, 0.0, NEG_FILL)


def weigh(scores, bias, group, before=None):
    peaks, weights = [], []
    for i in range(scores.shape[0] // group):
        piece = scores[i * group : (i + 1) * group] + bias[pl.ds(i, 1), :]
        peak = jnp.max(piece, axis=1, keepdims=True)
        if before is not None:
            peak = jnp.maximum(before[i], peak)
        peaks.append(peak)
        weights.append(jnp.exp(piece - peak).astype(jnp.bfloat16))
    return peaks, jnp.concatenate(weights, axis=0)


def near_kernel(
    cols, pool_blocks, count, line, position, q_up, q_down, bound, passed, keys, values, pool_keys, pool_values, near,
    qs, sums, tops, norms, numbers, ks, vs, tails, bias, sems,
):
    rows, width = qs.shape[0] // 2, qs.shape[1]
    group = rows // 2
    in_line = lax.rem(position[0], line)
    at_end = (in_line == 0, in_line == line - 1)
    near_keys, near_values = halves_of(near)
    blocks = [ref.at[pl.ds(i * group, group)] for ref in (q_up, q_down) for i in range(2)]
    copies = (
        fill(qs, blocks, sems, 0)
        + fill(ks, (keys, near_keys, pool_keys), sems, 4)
        + fill(vs, (values, near_values, pool_values), sems, 7)
    )
    for i in range(2):
        apart = fill(qs.at[pl.ds(i * rows, rows)], (bound.at[pl.ds(0, group)], passed), sems, 2 * i)
        corner = pl.ds(0, LANES)
        tail = tails.at[pl.ds(i * TILE, TILE)]
        source = (q_up, q_down)[i].at[pl.ds(rows, TILE), corner]
        copies.append(pltpu.make_async_copy(source, tail, sems.at[10 + i]))
        apart.append(pltpu.make_async_copy(bound.at[pl.ds(group, TILE), corner], tail, sems.at[10 + i]))

        @pl.when(at_end[i])
        def _():
            for copy in apart:
                copy.start()

        @pl.when(jnp.logical_not(at_end[i]))
        def _():
            for copy in (*copies[2 * i : 2 * i + 2], copies[10 + i]):
                copy.start()

    for copy in copies[4:10]:
        copy.start()
    for copy in copies:
        copy.wait()
    spot = Spot(position, cols, pool_blocks)
    for i in range(2):
        listed = numbers_of(tails[pl.ds(i * TILE, TILE), :], count)
        numbers[pl.ds(i * TILE, TILE), :] = listed
        bias[pl.ds(2 * i, 2), :] = bias_of(listed, spot, ks.shape[0], True, group, pool_keys.shape[0])[:2]
    scale = 1.0 / math.sqrt(width // HEADS)
    ones = jnp.ones((ks.shape[0], LANES), jnp.bfloat16)
    for head in range(HEADS):
        part = pl.ds(head * LANES, LANES)
        scores = lax.dot_general(qs[:, part], ks[:, part], NT, preferred_element_type=jnp.float32) * scale
        peaks, weights = weigh(scores, bias, group)
        value = jnp.concatenate([vs[:, part], ones], axis=1)
        summed = jnp.dot(weights, value, preferred_element_type=jnp.float32)
        sums[:, part] = summed[:, :LANES]
        norms[:, part] = summed[:, LANES:]
        for i, peak in enumerate(peaks):
            tops[pl.ds(i * group, group), part] = jnp.broadcast_to(peak, (group, LANES))


def near_attention(shape, position, q_up, q_down, bound, passed, keys, values, pool_keys, pool_values, near):
    rows, width = keys.shape
    total = rows + near.shape[0] // 2 + pool_keys.shape[0]
    bf16, f32 = jnp.bfloat16, jnp.float32
    held, sent = pltpu.HBM, pl.ANY
    places = (pltpu.SMEM, sent, sent, sent, sent, held, held, held, held, sent)
    return pl.pallas_call(
        functools.partial(near_kernel, *shape),
        out_shape=[jax.ShapeDtypeStruct((2 * rows, width), kind) for kind in (bf16, f32, f32, f32)]
        + [jax.ShapeDtypeStruct((2 * TILE, LANES), jnp.int32)],
        in_specs=[pl.BlockSpec(memory_space=place) for place in places],
        out_specs=[pl.BlockSpec(memory_space=pltpu.VMEM)] * 5,
        scratch_shapes=[
            pltpu.VMEM((total, width), bf16),
            pltpu.VMEM((total, width), bf16),
            pltpu.VMEM((2 * TILE, LANES), bf16),
            pltpu.VMEM((TILE, total), f32),
            pltpu.SemaphoreType.DMA((12,)),
        ],
        compiler_params=pltpu.CompilerParams(vmem_limit_bytes=11 << 20),
        cost_estimate=pl.CostEstimate(
            flops=4 * 2 * rows * total * width, bytes_accessed=4 << 20, transcendentals=2 * rows * total * HEADS
        ),
        name="near_attention",
    )(position, q_up, q_down, bound, passed, keys, values, pool_keys, pool_values, near)


def far_kernel(cols, pool_blocks, count, position, qs, sums, tops, norms, numbers, far, out_up, out_down, ks, vs, bias):
    edge = far.shape[0] // 2
    spot = Spot(position, cols, pool_blocks)
    half = out_up.shape[0] // 2
    for i in range(2):
        listed = numbers[pl.ds(i * TILE, TILE), :]
        bias[pl.ds(2 * i, 2), :] = bias_of(listed, spot, LANES, False, half, edge - half)[:2]
    rows = out_up.shape[0]
    width = qs.shape[1]
    group = rows // 2
    scale = 1.0 / math.sqrt(width // HEADS)
    for part, scratch in ((0, ks), (1, vs)):
        scratch[pl.ds(0, edge), :] = far[pl.ds(part * edge, edge), :]
        scratch[pl.ds(edge, LANES - edge), :] = jnp.zeros((LANES - edge, width), scratch.dtype)
    lane = lax.broadcasted_iota(jnp.int32, (group, LANES), 1)
    zero = jnp.zeros((group, LANES), jnp.float32)
    kept_peak, kept_norm = [zero] * 4, [zero + 1.0] * 4
    ones = jnp.ones((LANES, LANES), jnp.bfloat16)
    outs = (out_up, out_down)
    spans = [pl.ds(i * group, group) for i in range(4)]
    for head in range(HEADS):
        part = pl.ds(head * LANES, LANES)
        scores = lax.dot_general(qs[:, part], ks[:, part], NT, preferred_element_type=jnp.float32) * scale
        before = [tops[span, part] for span in spans]
        peaks, weights = weigh(scores, bias, group, before)
        value = jnp.concatenate([vs[:, part], ones], axis=1)
        summed = jnp.dot(weights, value, preferred_element_type=jnp.float32)
        for i, span in enumerate(spans):
            factor = jnp.exp(before[i] - peaks[i])
            piece = summed[i * group : (i + 1) * group]
            norm = norms[span, part] * factor + piece[:, LANES:]
            result = (sums[span, part] * factor + piece[:, :LANES]) / norm
            outs[i // 2][spans[i % 2], part] = result.astype(jnp.bfloat16)
            kept_peak[i] = jnp.where(lane == head, peaks[i], kept_peak[i])
            kept_norm[i] = jnp.where(lane == head, norm, kept_norm[i])
    for i in range(4):
        high, middle, low = split_in_three(kept_peak[i] + jnp.log(kept_norm[i]))
        middle = pltpu.roll(middle.astype(jnp.float32), HEADS, 1)
        low = pltpu.roll(low.astype(jnp.float32), 2 * HEADS, 1)
        outs[i // 2][spans[i % 2], pl.ds(width, LANES)] = (high.astype(jnp.float32) + middle + low).astype(jnp.bfloat16)


def far_attention(shape, position, qs, sums, tops, norms, numbers, far):
    rows, width = qs.shape[0] // 2, qs.shape[1]
    message = jax.ShapeDtypeStruct((rows, width + LANES), jnp.bfloat16)
    return pl.pallas_call(
        functools.partial(far_kernel, *shape),
        out_shape=(message, message),
        in_specs=[pl.BlockSpec(memory_space=pltpu.SMEM)] + [pl.BlockSpec(memory_space=pltpu.VMEM)] * 6,
        out_specs=[pl.BlockSpec(memory_space=pltpu.VMEM)] * 2,
        scratch_shapes=[pltpu.VMEM((LANES, width), jnp.bfloat16)] * 2 + [pltpu.VMEM((TILE, LANES), jnp.float32)],
        compiler_params=pltpu.CompilerParams(vmem_limit_bytes=3 << 20),
        cost_estimate=pl.CostEstimate(
            flops=4 * 2 * rows * LANES * width, bytes_accessed=4 << 20, transcendentals=2 * rows * LANES * HEADS
        ),
        name="far_attention",
    )(position, qs, sums, tops, norms, numbers, far)


def own_kernel(
    cols, pool_blocks, count, position, message, keys, values, pool_keys, pool_values, near, far, top_a, top_b,
    out, logs, qs, ks, vs, tail, bias, sems,
):
    rows, width = qs.shape
    group = rows // 2
    gap = ks.shape[0] - keys.shape[0] - near.shape[0] // 2 - pool_keys.shape[0] - far.shape[0] // 2 - 2 * top_a.shape[1]
    corner = message.at[pl.ds(rows, TILE), pl.ds(0, LANES)]
    copies = [
        pltpu.make_async_copy(message.at[pl.ds(0, rows)], qs, sems.at[0]),
        pltpu.make_async_copy(corner, tail, sems.at[13]),
    ]
    for part, scratch, mine, pool in ((0, ks, keys, pool_keys), (1, vs, values, pool_values)):
        spans = (top_a.at[part], top_b.at[part], mine, halves_of(near)[part], pool, halves_of(far)[part])
        copies += fill(scratch, spans, sems, 1 + 6 * part)
    for copy in copies:
        copy.start()
    for scratch in (ks, vs):
        scratch[pl.ds(ks.shape[0] - gap, gap), :] = jnp.zeros((gap, width), scratch.dtype)
    for copy in copies:
        copy.wait()
    spot = Spot(position, cols, pool_blocks)
    listed = numbers_of(tail[...], count)
    top, pool = 2 * top_a.shape[1], pool_keys.shape[0]
    chip = keys.shape[0] + near.shape[0] // 2 + pool
    bias[:, pl.ds(0, top)] = jnp.zeros((TILE, top), jnp.float32)
    bias[:, pl.ds(top, chip)] = bias_of(listed, spot, chip, True, group, pool)
    bias[:, pl.ds(top + chip, LANES)] = bias_of(listed, spot, LANES, False, group, pool)
    scale = 1.0 / math.sqrt(width // HEADS)
    ones = jnp.ones((ks.shape[0], LANES), jnp.bfloat16)
    for head in range(HEADS):
        part = pl.ds(head * LANES, LANES)
        scores = lax.dot_general(qs[:, part], ks[:, part], NT, preferred_element_type=jnp.float32) * scale
        peaks, weights = weigh(scores, bias, group)
        value = jnp.concatenate([vs[:, part], ones], axis=1)
        summed = jnp.dot(weights, value, preferred_element_type=jnp.float32)
        norm = summed[:, LANES:]
        out[:, part] = summed[:, :LANES] / norm
        for i, peak in enumerate(peaks):
            span = pl.ds(i * group, group)
            logs[span, part] = peak + jnp.log(norm[i * group : (i + 1) * group])


def own_attention(shape, position, message, keys, values, pool_keys, pool_values, near, far, top_a, top_b):
    rows, width = keys.shape
    total = 2 * top_a.shape[1] + rows + near.shape[0] // 2 + pool_keys.shape[0] + LANES
    bf16, f32 = jnp.bfloat16, jnp.float32
    held, sent = pltpu.HBM, pl.ANY
    places = (pltpu.SMEM, sent, held, held, held, held, sent, sent, sent, sent)
    return pl.pallas_call(
        functools.partial(own_kernel, *shape),
        out_shape=[jax.ShapeDtypeStruct((rows, width), f32)] * 2,
        in_specs=[pl.BlockSpec(memory_space=place) for place in places],
        out_specs=[pl.BlockSpec(memory_space=pltpu.VMEM)] * 2,
        scratch_shapes=[
            pltpu.VMEM((rows, width), bf16),
            pltpu.VMEM((total, width), bf16),
            pltpu.VMEM((total, width), bf16),
            pltpu.VMEM((TILE, LANES), bf16),
            pltpu.VMEM((TILE, total), f32),
            pltpu.SemaphoreType.DMA((14,)),
        ],
        compiler_params=pltpu.CompilerParams(vmem_limit_bytes=8 << 20),
        cost_estimate=pl.CostEstimate(
            flops=4 * rows * total * width, bytes_accessed=4 << 20, transcendentals=rows * total * HEADS
        ),
        name="own_attention",
    )(position, message, keys, values, pool_keys, pool_values, near, far, top_a, top_b)


def merge_kernel(last, position, own, own_logs, above, below, out):
    _, width = out.shape
    tail = pl.ds(width, LANES)
    logs = []
    for i, ref in enumerate((above, below)):
        coded = ref[:, tail].astype(jnp.float32)
        log = coded + pltpu.roll(coded, LANES - HEADS, 1) + pltpu.roll(coded, LANES - 2 * HEADS, 1)
        logs.append(jnp.where(position[0] == last * i, NEG_FILL, log))
    for head in range(HEADS):
        part = pl.ds(head * LANES, LANES)
        own_log = own_logs[:, part]
        up_log, down_log = (jnp.broadcast_to(log[:, head : head + 1], own_log.shape) for log in logs)
        peak = jnp.maximum(jnp.maximum(own_log, up_log), down_log)
        shares = [jnp.exp(log - peak) for log in (own_log, up_log, down_log)]
        result = own[:, part] * shares[0]
        result = result + above[:, part].astype(jnp.float32) * shares[1]
        result = result + below[:, part].astype(jnp.float32) * shares[2]
        out[:, part] = (result / (shares[0] + shares[1] + shares[2])).astype(out.dtype)


def merge(rows_in_all, position, own, own_logs, above, below):
    return pl.pallas_call(
        functools.partial(merge_kernel, rows_in_all - 1),
        out_shape=jax.ShapeDtypeStruct(own.shape, jnp.bfloat16),
        in_specs=[pl.BlockSpec(memory_space=pltpu.SMEM)] + [pl.BlockSpec(memory_space=pltpu.VMEM)] * 4,
        out_specs=pl.BlockSpec(memory_space=pltpu.VMEM),
        compiler_params=pltpu.CompilerParams(vmem_limit_bytes=4 << 20),
        name="merge",
    )(position, own, own_logs, above, below)


def body(queries, keys, values, pool_keys, pool_values, top_keys, top_values, coarse_ids):
    _, _, blocks, tokens, width = queries.shape
    pool_blocks, pool_tokens, _ = pool_keys.shape
    rows = lax.axis_size("row")
    cols = lax.axis_size("col")
    row = lax.axis_index("row")
    col = lax.axis_index("col")
    position = jnp.stack([row, col]).astype(jnp.int32)
    pool = pool_blocks * pool_tokens
    own = blocks * tokens

    up = pairs(rows, cols, lambda r, q: (r - 1, q))
    down = pairs(rows, cols, lambda r, q: (r + 1, q))
    partner = pairs(rows, cols, lambda r, q: (r, q ^ 1))
    across = pairs(rows, cols, lambda r, q: (r, q + 1 if q % 2 else q - 1))
    line = rows // 4
    nowhere = (-1, -1)
    at_start = lambda r: r % line == 0
    at_end = lambda r: r % line == line - 1
    up_inside = pairs(rows, cols, lambda r, q: nowhere if at_start(r) else (r - 1, q))
    down_inside = pairs(rows, cols, lambda r, q: nowhere if at_end(r) else (r + 1, q))
    between = pairs(rows, cols, lambda r, q: (r + 1, q) if at_end(r) else (r - 1, q) if at_start(r) else nowhere)
    along_z = pairs(rows, cols, lambda r, q: (r + line, q) if at_end(r) else (r - line, q) if at_start(r) else nowhere)
    round_y = pairs(
        rows,
        cols,
        lambda r, q: (r - line + 1, q)
        if at_end(r) and r >= line
        else (r + line - 1, q)
        if at_start(r) and r < rows - line
        else nowhere,
    )
    halves = pairs(rows, cols, lambda r, q: ((3 - r // line) * line + r % line, q ^ 2))
    step_one = pairs(rows, cols, lambda r, q: (r, q ^ 4))
    step_two = pairs(rows, cols, lambda r, q: (r, q ^ 8))

    def stay(array, *shape):
        return pltpu.with_memory_space_constraint(array.reshape(shape), pltpu.HBM)

    pk = stay(pool_keys, pool, width)
    pv = stay(pool_values, pool, width)
    sources = (
        stay(queries, blocks, tokens, width),
        stay(keys, blocks, tokens, width),
        stay(values, blocks, tokens, width),
        pk,
        pv,
    )
    shares = (stay(top_keys, *top_keys.shape[1:]), stay(top_values, *top_values.shape[1:]))
    ids = coarse_ids.reshape(blocks, -1)
    edge = (2 * (tokens + pool), width)
    far, second = packed(pack_far_kernel, [edge, (tokens, width)], [position], sources, 5)
    passed = send(second, along_z)
    far = send(far, across)
    near, top, message, bound = packed(
        pack_near_kernel,
        [edge, (2,) + top_keys.shape[1:], (own + TILE, width), (tokens + TILE, width)],
        [position, ids],
        sources + shares,
        9,
    )
    bound = send(bound, between)
    q_down = send(message, up_inside)
    q_up = send(message, down_inside)
    near = send(near, partner)
    passed = send(passed, round_y)
    for links in (step_one, step_two, halves):
        top = join(top, send(top, links))
    top_other = send(top, partner)

    shape = (cols, pool_blocks, ids.shape[1])
    kept_keys, kept_values = stay(keys, own, width), stay(values, own, width)
    near_parts = near_attention(
        shape + (line,), position, q_up, q_down, bound, passed, kept_keys, kept_values, pk, pv, near
    )
    to_up, to_down = far_attention(shape, position, *near_parts, far)
    below = send(to_up, up)
    above = send(to_down, down)
    mine = own_attention(shape, position, message, kept_keys, kept_values, pk, pv, near, far, top, top_other)
    return merge(rows, position, *mine, above, below).reshape(queries.shape)


def solution(mesh):
    placed = (
        P(None, "row", "col", None, None),
        P(None, "row", "col", None, None),
        P(None, "row", "col", None, None),
        P(("row", "col"), None, None),
        P(("row", "col"), None, None),
        P(None, "col", None),
        P(None, "col", None),
        P(None, "row", "col", None),
    )

    return jax.shard_map(
        body,
        mesh=mesh,
        in_specs=placed,
        out_specs=P(None, "row", "col", None, None),
        check_vma=False,
    )
```

```python
import functools
import math

import jax
import jax.numpy as jnp
from jax import lax
from jax.experimental import pallas as pl
from jax.experimental.pallas import tpu as pltpu
from jax.sharding import PartitionSpec as P


HEADS = 16
NEG_FILL = -1e30
AXES = ("row", "col")
LANES = 128
TILE = 8
BASE = 256


def pairs(rows, cols, target):
    out = []
    for row in range(rows):
        for col in range(cols):
            there = target(row, col)
            if 0 <= there[0] < rows and 0 <= there[1] < cols:
                out.append((row * cols + col, there[0] * cols + there[1]))
    return out


def send(block, links):
    return lax.ppermute(block, AXES, links)


def into(out, sources):
    copies, place = [], 0
    for ref in sources:
        copies.append((ref, out.at[pl.ds(place, ref.shape[0])]))
        place += ref.shape[0]
    return copies


def carry_out(copies, sems):
    run([pltpu.make_async_copy(a, b, sems.at[i]) for i, (a, b) in enumerate(copies)])


def pack_far_kernel(position, query, keys, values, pool_keys, pool_values, far, second, sems):
    block = lax.rem(position[1], 2)
    copies = into(far, (keys.at[block], pool_keys, values.at[block], pool_values))
    carry_out(copies + [(query.at[1], second)], sems)


def pack_near_kernel(
    position, ids, query, keys, values, pool_keys, pool_values, top_keys, top_values, near, top, message, bound, sems
):
    block = 1 - lax.rem(position[1], 2)
    blocks, _, _ = query.shape
    copies = into(near, (keys.at[block], pool_keys, values.at[block], pool_values))
    copies += [(top_keys, top.at[0]), (top_values, top.at[1])]
    copies += into(message, [query.at[i] for i in range(blocks)])
    copies += into(bound, [query.at[0]])
    started = [pltpu.make_async_copy(a, b, sems.at[i]) for i, (a, b) in enumerate(copies)]
    for copy in started:
        copy.start()
    count = ids.shape[1]
    line = lax.broadcasted_iota(jnp.int32, (TILE, LANES), 0)
    lane = lax.broadcasted_iota(jnp.int32, (TILE, LANES), 1)
    digits = jnp.zeros((TILE, LANES), jnp.int32)
    for i in range(blocks):
        for j in range(count):
            number = ids[i, j]
            digits = jnp.where((line == i) & (lane == j), number // BASE, digits)
            digits = jnp.where((line == i) & (lane == count + j), number % BASE, digits)
    digits = digits.astype(jnp.float32).astype(message.dtype)
    for out in (message, bound):
        tail = pl.ds(out.shape[0] - TILE, TILE)
        out[tail, :] = jnp.zeros((TILE, out.shape[1]), out.dtype)
        out[tail, pl.ds(0, LANES)] = digits
    for copy in started:
        copy.wait()


def join_kernel(first, second, out, sems):
    size = first.shape[1]
    pieces = []
    for i in range(2):
        pieces.append((first.at[i], out.at[i, pl.ds(0, size)]))
        pieces.append((second.at[i], out.at[i, pl.ds(size, size)]))
    carry_out(pieces, sems)


def join(first, second):
    shape = (2, 2 * first.shape[1], first.shape[2])
    return pl.pallas_call(
        join_kernel,
        out_shape=jax.ShapeDtypeStruct(shape, first.dtype),
        in_specs=[pl.BlockSpec(memory_space=pl.ANY)] * 2,
        out_specs=pl.BlockSpec(memory_space=pltpu.VMEM),
        scratch_shapes=[pltpu.SemaphoreType.DMA((4,))],
        compiler_params=pltpu.CompilerParams(vmem_limit_bytes=1 << 20),
        name="join",
    )(first, second)


def packed(kernel, outs, scalars, arrays, copies):
    dtype = arrays[0].dtype
    places = [pltpu.SMEM] * len(scalars) + [pltpu.HBM] * len(arrays)
    return pl.pallas_call(
        kernel,
        out_shape=[jax.ShapeDtypeStruct(shape, dtype) for shape in outs],
        in_specs=[pl.BlockSpec(memory_space=place) for place in places],
        out_specs=[pl.BlockSpec(memory_space=pltpu.VMEM)] * len(outs),
        scratch_shapes=[pltpu.SemaphoreType.DMA((copies,))],
        compiler_params=pltpu.CompilerParams(vmem_limit_bytes=4 << 20),
    )(*scalars, *arrays)


def split_in_three(value):
    high = value.astype(jnp.bfloat16)
    rest = value - high.astype(jnp.float32)
    middle = rest.astype(jnp.bfloat16)
    low = (rest - middle.astype(jnp.float32)).astype(jnp.bfloat16)
    return high, middle, low


NT = (((1,), (1,)), ((), ()))


def fill(scratch, spans, sems, first):
    copies = []
    place = 0
    for ref in spans:
        count = ref.shape[0]
        copies.append(pltpu.make_async_copy(ref, scratch.at[pl.ds(place, count)], sems.at[first + len(copies)]))
        place += count
    return copies


def halves_of(ref):
    edge = ref.shape[0] // 2
    return ref.at[pl.ds(0, edge)], ref.at[pl.ds(edge, edge)]


def run(copies):
    for copy in copies:
        copy.start()
    for copy in copies:
        copy.wait()


class Spot:
    def __init__(self, position, cols, blocks):
        row, col = position[0], position[1]
        self.side = lax.rem(col, 2)
        other = col + 1 - 2 * self.side
        beyond = col - 1 + 2 * self.side
        self.exists = jnp.where((beyond >= 0) & (beyond < cols), 1, 0)
        self.own, self.other, self.beyond = ((row * cols + holder) * blocks for holder in (col, other, beyond))
        self.blocks = blocks


def numbers_of(digits, count):
    digits = digits.astype(jnp.float32)
    lane = lax.broadcasted_iota(jnp.int32, digits.shape, 1)
    number = digits * BASE + pltpu.roll(digits, LANES - count, 1)
    return jnp.where(lane < count, number, -1.0).astype(jnp.int32)


def bias_of(numbers, spot, width, near, tokens, pool):
    lane = lax.broadcasted_iota(jnp.int32, (TILE, width), 1)
    line = lax.broadcasted_iota(jnp.int32, (TILE, width), 0)
    if near:
        start = 2 * tokens
        mine = jnp.where(line == 1 - spot.side, 1, 0)
        listed = jnp.where(lane < start, 1, 0)
        holders = (spot.other, spot.own)
    else:
        start = 0
        mine = jnp.where(line == spot.side, spot.exists, 0)
        listed = jnp.zeros((TILE, width), jnp.int32)
        holders = (spot.beyond,)
    listed = jnp.where((lane >= start) & (lane < start + tokens), mine, listed)
    start += tokens
    size = pool // spot.blocks
    for holder in holders:
        for i in range(spot.blocks):
            hit = jnp.max(jnp.where(numbers == holder + i, 1.0, 0.0), axis=1, keepdims=True)
            hit = jnp.broadcast_to(hit, (TILE, width)).astype(jnp.int32)
            if not near:
                hit = hit * spot.exists
            listed = jnp.where((lane >= start) & (lane < start + size), hit, listed)
            start += size
    return jnp.where(listed > 0, 0.0, NEG_FILL)


def weigh(scores, bias, group, before=None):
    peaks, weights = [], []
    for i in range(scores.shape[0] // group):
        piece = scores[i * group : (i + 1) * group] + bias[pl.ds(i, 1), :]
        peak = jnp.max(piece, axis=1, keepdims=True)
        if before is not None:
            peak = jnp.maximum(before[i], peak)
        peaks.append(peak)
        weights.append(jnp.exp(piece - peak).astype(jnp.bfloat16))
    return peaks, jnp.concatenate(weights, axis=0)


def near_kernel(
    cols, pool_blocks, count, line, position, q_up, q_down, bound, passed, keys, values, pool_keys, pool_values, near,
    qs, sums, tops, norms, far_bias, ks, vs, tails, bias, sems,
):
    rows, width = qs.shape[0] // 2, qs.shape[1]
    group = rows // 2
    in_line = lax.rem(position[0], line)
    at_end = (in_line == 0, in_line == line - 1)
    near_keys, near_values = halves_of(near)
    blocks = [ref.at[pl.ds(i * group, group)] for ref in (q_up, q_down) for i in range(2)]
    copies = (
        fill(qs, blocks, sems, 0)
        + fill(ks, (keys, near_keys, pool_keys), sems, 4)
        + fill(vs, (values, near_values, pool_values), sems, 7)
    )
    for i in range(2):
        apart = fill(qs.at[pl.ds(i * rows, rows)], (bound.at[pl.ds(0, group)], passed), sems, 2 * i)
        corner = pl.ds(0, LANES)
        tail = tails.at[pl.ds(i * TILE, TILE)]
        source = (q_up, q_down)[i].at[pl.ds(rows, TILE), corner]
        copies.append(pltpu.make_async_copy(source, tail, sems.at[10 + i]))
        apart.append(pltpu.make_async_copy(bound.at[pl.ds(group, TILE), corner], tail, sems.at[10 + i]))

        @pl.when(at_end[i])
        def _():
            for copy in apart:
                copy.start()

        @pl.when(jnp.logical_not(at_end[i]))
        def _():
            for copy in (*copies[2 * i : 2 * i + 2], copies[10 + i]):
                copy.start()

    for copy in copies[4:10]:
        copy.start()
    for copy in copies:
        copy.wait()
    spot = Spot(position, cols, pool_blocks)
    for i in range(2):
        listed = numbers_of(tails[pl.ds(i * TILE, TILE), :], count)
        bias[pl.ds(2 * i, 2), :] = bias_of(listed, spot, ks.shape[0], True, group, pool_keys.shape[0])[:2]
        far_bias[pl.ds(2 * i, 2), :] = bias_of(listed, spot, LANES, False, group, pool_keys.shape[0])[:2]
    scale = 1.0 / math.sqrt(width // HEADS)
    ones = jnp.ones((ks.shape[0], LANES), jnp.bfloat16)
    for head in range(HEADS):
        part = pl.ds(head * LANES, LANES)
        scores = lax.dot_general(qs[:, part], ks[:, part], NT, preferred_element_type=jnp.float32) * scale
        peaks, weights = weigh(scores, bias, group)
        value = jnp.concatenate([vs[:, part], ones], axis=1)
        summed = jnp.dot(weights, value, preferred_element_type=jnp.float32)
        sums[:, part] = summed[:, :LANES]
        norms[:, part] = summed[:, LANES:]
        for i, peak in enumerate(peaks):
            tops[pl.ds(i * group, group), part] = jnp.broadcast_to(peak, (group, LANES))


def near_attention(shape, position, q_up, q_down, bound, passed, keys, values, pool_keys, pool_values, near):
    rows, width = keys.shape
    total = rows + near.shape[0] // 2 + pool_keys.shape[0]
    bf16, f32 = jnp.bfloat16, jnp.float32
    held, sent = pltpu.HBM, pl.ANY
    places = (pltpu.SMEM, sent, sent, sent, sent, held, held, held, held, sent)
    return pl.pallas_call(
        functools.partial(near_kernel, *shape),
        out_shape=[jax.ShapeDtypeStruct((2 * rows, width), kind) for kind in (bf16, f32, f32, f32)]
        + [jax.ShapeDtypeStruct((TILE, LANES), f32)],
        in_specs=[pl.BlockSpec(memory_space=place) for place in places],
        out_specs=[pl.BlockSpec(memory_space=pltpu.VMEM)] * 5,
        scratch_shapes=[
            pltpu.VMEM((total, width), bf16),
            pltpu.VMEM((total, width), bf16),
            pltpu.VMEM((2 * TILE, LANES), bf16),
            pltpu.VMEM((TILE, total), f32),
            pltpu.SemaphoreType.DMA((12,)),
        ],
        compiler_params=pltpu.CompilerParams(vmem_limit_bytes=11 << 20),
        cost_estimate=pl.CostEstimate(
            flops=4 * 2 * rows * total * width, bytes_accessed=4 << 20, transcendentals=2 * rows * total * HEADS
        ),
        name="near_attention",
    )(position, q_up, q_down, bound, passed, keys, values, pool_keys, pool_values, near)


def far_kernel(qs, sums, tops, norms, bias, far, out_up, out_down, ks, vs):
    edge = far.shape[0] // 2
    rows = out_up.shape[0]
    width = qs.shape[1]
    group = rows // 2
    scale = 1.0 / math.sqrt(width // HEADS)
    for part, scratch in ((0, ks), (1, vs)):
        scratch[pl.ds(0, edge), :] = far[pl.ds(part * edge, edge), :]
        scratch[pl.ds(edge, LANES - edge), :] = jnp.zeros((LANES - edge, width), scratch.dtype)
    lane = lax.broadcasted_iota(jnp.int32, (group, LANES), 1)
    zero = jnp.zeros((group, LANES), jnp.float32)
    kept_peak, kept_norm = [zero] * 4, [zero + 1.0] * 4
    ones = jnp.ones((LANES, LANES), jnp.bfloat16)
    outs = (out_up, out_down)
    spans = [pl.ds(i * group, group) for i in range(4)]
    for head in range(HEADS):
        part = pl.ds(head * LANES, LANES)
        scores = lax.dot_general(qs[:, part], ks[:, part], NT, preferred_element_type=jnp.float32) * scale
        before = [tops[span, part] for span in spans]
        peaks, weights = weigh(scores, bias, group, before)
        value = jnp.concatenate([vs[:, part], ones], axis=1)
        summed = jnp.dot(weights, value, preferred_element_type=jnp.float32)
        for i, span in enumerate(spans):
            factor = jnp.exp(before[i] - peaks[i])
            piece = summed[i * group : (i + 1) * group]
            norm = norms[span, part] * factor + piece[:, LANES:]
            result = (sums[span, part] * factor + piece[:, :LANES]) / norm
            outs[i // 2][spans[i % 2], part] = result.astype(jnp.bfloat16)
            kept_peak[i] = jnp.where(lane == head, peaks[i], kept_peak[i])
            kept_norm[i] = jnp.where(lane == head, norm, kept_norm[i])
    for i in range(4):
        high, middle, low = split_in_three(kept_peak[i] + jnp.log(kept_norm[i]))
        middle = pltpu.roll(middle.astype(jnp.float32), HEADS, 1)
        low = pltpu.roll(low.astype(jnp.float32), 2 * HEADS, 1)
        outs[i // 2][spans[i % 2], pl.ds(width, LANES)] = (high.astype(jnp.float32) + middle + low).astype(jnp.bfloat16)


def far_attention(qs, sums, tops, norms, bias, far):
    rows, width = qs.shape[0] // 2, qs.shape[1]
    message = jax.ShapeDtypeStruct((rows, width + LANES), jnp.bfloat16)
    return pl.pallas_call(
        far_kernel,
        out_shape=(message, message),
        in_specs=[pl.BlockSpec(memory_space=pltpu.VMEM)] * 6,
        out_specs=[pl.BlockSpec(memory_space=pltpu.VMEM)] * 2,
        scratch_shapes=[pltpu.VMEM((LANES, width), jnp.bfloat16)] * 2,
        compiler_params=pltpu.CompilerParams(vmem_limit_bytes=3 << 20),
        cost_estimate=pl.CostEstimate(
            flops=4 * 2 * rows * LANES * width, bytes_accessed=4 << 20, transcendentals=2 * rows * LANES * HEADS
        ),
        name="far_attention",
    )(qs, sums, tops, norms, bias, far)


def own_kernel(
    cols, pool_blocks, count, position, message, keys, values, pool_keys, pool_values, near, far, top_a, top_b,
    out, logs, qs, ks, vs, tail, bias, sems,
):
    rows, width = qs.shape
    group = rows // 2
    gap = ks.shape[0] - keys.shape[0] - near.shape[0] // 2 - pool_keys.shape[0] - far.shape[0] // 2 - 2 * top_a.shape[1]
    corner = message.at[pl.ds(rows, TILE), pl.ds(0, LANES)]
    copies = [
        pltpu.make_async_copy(message.at[pl.ds(0, rows)], qs, sems.at[0]),
        pltpu.make_async_copy(corner, tail, sems.at[13]),
    ]
    for part, scratch, mine, pool in ((0, ks, keys, pool_keys), (1, vs, values, pool_values)):
        spans = (top_a.at[part], top_b.at[part], mine, halves_of(near)[part], pool, halves_of(far)[part])
        copies += fill(scratch, spans, sems, 1 + 6 * part)
    for copy in copies:
        copy.start()
    for scratch in (ks, vs):
        scratch[pl.ds(ks.shape[0] - gap, gap), :] = jnp.zeros((gap, width), scratch.dtype)
    for copy in copies:
        copy.wait()
    spot = Spot(position, cols, pool_blocks)
    listed = numbers_of(tail[...], count)
    top, pool = 2 * top_a.shape[1], pool_keys.shape[0]
    chip = keys.shape[0] + near.shape[0] // 2 + pool
    bias[:, pl.ds(0, top)] = jnp.zeros((TILE, top), jnp.float32)
    bias[:, pl.ds(top, chip)] = bias_of(listed, spot, chip, True, group, pool)
    bias[:, pl.ds(top + chip, LANES)] = bias_of(listed, spot, LANES, False, group, pool)
    scale = 1.0 / math.sqrt(width // HEADS)
    ones = jnp.ones((ks.shape[0], LANES), jnp.bfloat16)
    for head in range(HEADS):
        part = pl.ds(head * LANES, LANES)
        scores = lax.dot_general(qs[:, part], ks[:, part], NT, preferred_element_type=jnp.float32) * scale
        peaks, weights = weigh(scores, bias, group)
        value = jnp.concatenate([vs[:, part], ones], axis=1)
        summed = jnp.dot(weights, value, preferred_element_type=jnp.float32)
        norm = summed[:, LANES:]
        out[:, part] = summed[:, :LANES] / norm
        for i, peak in enumerate(peaks):
            span = pl.ds(i * group, group)
            logs[span, part] = peak + jnp.log(norm[i * group : (i + 1) * group])


def own_attention(shape, position, message, keys, values, pool_keys, pool_values, near, far, top_a, top_b):
    rows, width = keys.shape
    total = 2 * top_a.shape[1] + rows + near.shape[0] // 2 + pool_keys.shape[0] + LANES
    bf16, f32 = jnp.bfloat16, jnp.float32
    held, sent = pltpu.HBM, pl.ANY
    places = (pltpu.SMEM, sent, held, held, held, held, sent, sent, sent, sent)
    return pl.pallas_call(
        functools.partial(own_kernel, *shape),
        out_shape=[jax.ShapeDtypeStruct((rows, width), f32)] * 2,
        in_specs=[pl.BlockSpec(memory_space=place) for place in places],
        out_specs=[pl.BlockSpec(memory_space=pltpu.VMEM)] * 2,
        scratch_shapes=[
            pltpu.VMEM((rows, width), bf16),
            pltpu.VMEM((total, width), bf16),
            pltpu.VMEM((total, width), bf16),
            pltpu.VMEM((TILE, LANES), bf16),
            pltpu.VMEM((TILE, total), f32),
            pltpu.SemaphoreType.DMA((14,)),
        ],
        compiler_params=pltpu.CompilerParams(vmem_limit_bytes=8 << 20),
        cost_estimate=pl.CostEstimate(
            flops=4 * rows * total * width, bytes_accessed=4 << 20, transcendentals=rows * total * HEADS
        ),
        name="own_attention",
    )(position, message, keys, values, pool_keys, pool_values, near, far, top_a, top_b)


def merge_kernel(last, position, own, own_logs, above, below, out):
    _, width = out.shape
    tail = pl.ds(width, LANES)
    logs = []
    for i, ref in enumerate((above, below)):
        coded = ref[:, tail].astype(jnp.float32)
        log = coded + pltpu.roll(coded, LANES - HEADS, 1) + pltpu.roll(coded, LANES - 2 * HEADS, 1)
        logs.append(jnp.where(position[0] == last * i, NEG_FILL, log))
    for head in range(HEADS):
        part = pl.ds(head * LANES, LANES)
        own_log = own_logs[:, part]
        up_log, down_log = (jnp.broadcast_to(log[:, head : head + 1], own_log.shape) for log in logs)
        peak = jnp.maximum(jnp.maximum(own_log, up_log), down_log)
        shares = [jnp.exp(log - peak) for log in (own_log, up_log, down_log)]
        result = own[:, part] * shares[0]
        result = result + above[:, part].astype(jnp.float32) * shares[1]
        result = result + below[:, part].astype(jnp.float32) * shares[2]
        out[:, part] = (result / (shares[0] + shares[1] + shares[2])).astype(out.dtype)


def merge(rows_in_all, position, own, own_logs, above, below):
    return pl.pallas_call(
        functools.partial(merge_kernel, rows_in_all - 1),
        out_shape=jax.ShapeDtypeStruct(own.shape, jnp.bfloat16),
        in_specs=[pl.BlockSpec(memory_space=pltpu.SMEM)] + [pl.BlockSpec(memory_space=pltpu.VMEM)] * 4,
        out_specs=pl.BlockSpec(memory_space=pltpu.VMEM),
        compiler_params=pltpu.CompilerParams(vmem_limit_bytes=4 << 20),
        name="merge",
    )(position, own, own_logs, above, below)


def body(queries, keys, values, pool_keys, pool_values, top_keys, top_values, coarse_ids):
    _, _, blocks, tokens, width = queries.shape
    pool_blocks, pool_tokens, _ = pool_keys.shape
    rows = lax.axis_size("row")
    cols = lax.axis_size("col")
    row = lax.axis_index("row")
    col = lax.axis_index("col")
    position = jnp.stack([row, col]).astype(jnp.int32)
    pool = pool_blocks * pool_tokens
    own = blocks * tokens

    up = pairs(rows, cols, lambda r, q: (r - 1, q))
    down = pairs(rows, cols, lambda r, q: (r + 1, q))
    partner = pairs(rows, cols, lambda r, q: (r, q ^ 1))
    across = pairs(rows, cols, lambda r, q: (r, q + 1 if q % 2 else q - 1))
    line = rows // 4
    nowhere = (-1, -1)
    at_start = lambda r: r % line == 0
    at_end = lambda r: r % line == line - 1
    up_inside = pairs(rows, cols, lambda r, q: nowhere if at_start(r) else (r - 1, q))
    down_inside = pairs(rows, cols, lambda r, q: nowhere if at_end(r) else (r + 1, q))
    between = pairs(rows, cols, lambda r, q: (r + 1, q) if at_end(r) else (r - 1, q) if at_start(r) else nowhere)
    along_z = pairs(rows, cols, lambda r, q: (r + line, q) if at_end(r) else (r - line, q) if at_start(r) else nowhere)
    round_y = pairs(
        rows,
        cols,
        lambda r, q: (r - line + 1, q)
        if at_end(r) and r >= line
        else (r + line - 1, q)
        if at_start(r) and r < rows - line
        else nowhere,
    )
    halves = pairs(rows, cols, lambda r, q: ((3 - r // line) * line + r % line, q ^ 2))
    step_one = pairs(rows, cols, lambda r, q: (r, q ^ 4))
    step_two = pairs(rows, cols, lambda r, q: (r, q ^ 8))

    def stay(array, *shape):
        return pltpu.with_memory_space_constraint(array.reshape(shape), pltpu.HBM)

    pk = stay(pool_keys, pool, width)
    pv = stay(pool_values, pool, width)
    sources = (
        stay(queries, blocks, tokens, width),
        stay(keys, blocks, tokens, width),
        stay(values, blocks, tokens, width),
        pk,
        pv,
    )
    shares = (stay(top_keys, *top_keys.shape[1:]), stay(top_values, *top_values.shape[1:]))
    ids = coarse_ids.reshape(blocks, -1)
    edge = (2 * (tokens + pool), width)
    far, second = packed(pack_far_kernel, [edge, (tokens, width)], [position], sources, 5)
    passed = send(second, along_z)
    far = send(far, across)
    near, top, message, bound = packed(
        pack_near_kernel,
        [edge, (2,) + top_keys.shape[1:], (own + TILE, width), (tokens + TILE, width)],
        [position, ids],
        sources + shares,
        9,
    )
    bound = send(bound, between)
    q_down = send(message, up_inside)
    q_up = send(message, down_inside)
    near = send(near, partner)
    passed = send(passed, round_y)
    for links in (step_one, step_two, halves):
        top = join(top, send(top, links))
    top_other = send(top, partner)

    shape = (cols, pool_blocks, ids.shape[1])
    kept_keys, kept_values = stay(keys, own, width), stay(values, own, width)
    near_parts = near_attention(
        shape + (line,), position, q_up, q_down, bound, passed, kept_keys, kept_values, pk, pv, near
    )
    to_up, to_down = far_attention(*near_parts, far)
    below = send(to_up, up)
    above = send(to_down, down)
    mine = own_attention(shape, position, message, kept_keys, kept_values, pk, pv, near, far, top, top_other)
    return merge(rows, position, *mine, above, below).reshape(queries.shape)


def solution(mesh):
    placed = (
        P(None, "row", "col", None, None),
        P(None, "row", "col", None, None),
        P(None, "row", "col", None, None),
        P(("row", "col"), None, None),
        P(("row", "col"), None, None),
        P(None, "col", None),
        P(None, "col", None),
        P(None, "row", "col", None),
    )

    return jax.shard_map(
        body,
        mesh=mesh,
        in_specs=placed,
        out_specs=P(None, "row", "col", None, None),
        check_vma=False,
    )
```

```python
import functools
import math

import jax
import jax.numpy as jnp
from jax import lax
from jax.experimental import pallas as pl
from jax.experimental.pallas import tpu as pltpu
from jax.sharding import PartitionSpec as P


HEADS = 16
NEG_FILL = -1e30
AXES = ("row", "col")
LANES = 128
LOG2E = math.log2(math.e)
TILE = 8
BASE = 256


def pairs(rows, cols, target):
    out = []
    for row in range(rows):
        for col in range(cols):
            there = target(row, col)
            if 0 <= there[0] < rows and 0 <= there[1] < cols:
                out.append((row * cols + col, there[0] * cols + there[1]))
    return out


def send(block, links):
    return lax.ppermute(block, AXES, links)


def into(out, sources):
    copies, place = [], 0
    for ref in sources:
        copies.append((ref, out.at[pl.ds(place, ref.shape[0])]))
        place += ref.shape[0]
    return copies


def carry_out(copies, sems):
    run([pltpu.make_async_copy(a, b, sems.at[i]) for i, (a, b) in enumerate(copies)])


def pack_far_kernel(position, query, keys, values, pool_keys, pool_values, far, second, sems):
    block = lax.rem(position[1], 2)
    copies = into(far, (keys.at[block], pool_keys, values.at[block], pool_values))
    carry_out(copies + [(query.at[1], second)], sems)


def pack_near_kernel(
    position, ids, query, keys, values, pool_keys, pool_values, top_keys, top_values, near, top, message, bound, sems
):
    block = 1 - lax.rem(position[1], 2)
    blocks, _, _ = query.shape
    copies = into(near, (keys.at[block], pool_keys, values.at[block], pool_values))
    copies += [(top_keys, top.at[0]), (top_values, top.at[1])]
    copies += into(message, [query.at[i] for i in range(blocks)])
    copies += into(bound, [query.at[0]])
    started = [pltpu.make_async_copy(a, b, sems.at[i]) for i, (a, b) in enumerate(copies)]
    for copy in started:
        copy.start()
    count = ids.shape[1]
    line = lax.broadcasted_iota(jnp.int32, (TILE, LANES), 0)
    lane = lax.broadcasted_iota(jnp.int32, (TILE, LANES), 1)
    digits = jnp.zeros((TILE, LANES), jnp.int32)
    for i in range(blocks):
        for j in range(count):
            number = ids[i, j]
            digits = jnp.where((line == i) & (lane == j), number // BASE, digits)
            digits = jnp.where((line == i) & (lane == count + j), number % BASE, digits)
    digits = digits.astype(jnp.float32).astype(message.dtype)
    for out in (message, bound):
        tail = pl.ds(out.shape[0] - TILE, TILE)
        out[tail, :] = jnp.zeros((TILE, out.shape[1]), out.dtype)
        out[tail, pl.ds(0, LANES)] = digits
    for copy in started:
        copy.wait()


def join_kernel(first, second, out, sems):
    size = first.shape[1]
    pieces = []
    for i in range(2):
        pieces.append((first.at[i], out.at[i, pl.ds(0, size)]))
        pieces.append((second.at[i], out.at[i, pl.ds(size, size)]))
    carry_out(pieces, sems)


def join(first, second):
    shape = (2, 2 * first.shape[1], first.shape[2])
    return pl.pallas_call(
        join_kernel,
        out_shape=jax.ShapeDtypeStruct(shape, first.dtype),
        in_specs=[pl.BlockSpec(memory_space=pl.ANY)] * 2,
        out_specs=pl.BlockSpec(memory_space=pltpu.VMEM),
        scratch_shapes=[pltpu.SemaphoreType.DMA((4,))],
        compiler_params=pltpu.CompilerParams(vmem_limit_bytes=1 << 20),
        name="join",
    )(first, second)


def packed(kernel, outs, scalars, arrays, copies):
    dtype = arrays[0].dtype
    places = [pltpu.SMEM] * len(scalars) + [pltpu.HBM] * len(arrays)
    return pl.pallas_call(
        kernel,
        out_shape=[jax.ShapeDtypeStruct(shape, dtype) for shape in outs],
        in_specs=[pl.BlockSpec(memory_space=place) for place in places],
        out_specs=[pl.BlockSpec(memory_space=pltpu.VMEM)] * len(outs),
        scratch_shapes=[pltpu.SemaphoreType.DMA((copies,))],
        compiler_params=pltpu.CompilerParams(vmem_limit_bytes=4 << 20),
    )(*scalars, *arrays)


def split_in_three(value):
    high = value.astype(jnp.bfloat16)
    rest = value - high.astype(jnp.float32)
    middle = rest.astype(jnp.bfloat16)
    low = (rest - middle.astype(jnp.float32)).astype(jnp.bfloat16)
    return high, middle, low


NT = (((1,), (1,)), ((), ()))


def fill(scratch, spans, sems, first):
    copies = []
    place = 0
    for ref in spans:
        count = ref.shape[0]
        copies.append(pltpu.make_async_copy(ref, scratch.at[pl.ds(place, count)], sems.at[first + len(copies)]))
        place += count
    return copies


def halves_of(ref):
    edge = ref.shape[0] // 2
    return ref.at[pl.ds(0, edge)], ref.at[pl.ds(edge, edge)]


def run(copies):
    for copy in copies:
        copy.start()
    for copy in copies:
        copy.wait()


class Spot:
    def __init__(self, position, cols, blocks):
        row, col = position[0], position[1]
        self.side = lax.rem(col, 2)
        other = col + 1 - 2 * self.side
        beyond = col - 1 + 2 * self.side
        self.exists = jnp.where((beyond >= 0) & (beyond < cols), 1, 0)
        self.own, self.other, self.beyond = ((row * cols + holder) * blocks for holder in (col, other, beyond))
        self.blocks = blocks


def numbers_of(digits, count):
    digits = digits.astype(jnp.float32)
    lane = lax.broadcasted_iota(jnp.int32, digits.shape, 1)
    number = digits * BASE + pltpu.roll(digits, LANES - count, 1)
    return jnp.where(lane < count, number, -1.0).astype(jnp.int32)


def bias_of(numbers, spot, width, near, tokens, pool):
    lane = lax.broadcasted_iota(jnp.int32, (TILE, width), 1)
    line = lax.broadcasted_iota(jnp.int32, (TILE, width), 0)
    if near:
        start = 2 * tokens
        mine = jnp.where(line == 1 - spot.side, 1, 0)
        listed = jnp.where(lane < start, 1, 0)
        holders = (spot.other, spot.own)
    else:
        start = 0
        mine = jnp.where(line == spot.side, spot.exists, 0)
        listed = jnp.zeros((TILE, width), jnp.int32)
        holders = (spot.beyond,)
    listed = jnp.where((lane >= start) & (lane < start + tokens), mine, listed)
    start += tokens
    size = pool // spot.blocks
    for holder in holders:
        for i in range(spot.blocks):
            hit = jnp.max(jnp.where(numbers == holder + i, 1.0, 0.0), axis=1, keepdims=True)
            hit = jnp.broadcast_to(hit, (TILE, width)).astype(jnp.int32)
            if not near:
                hit = hit * spot.exists
            listed = jnp.where((lane >= start) & (lane < start + size), hit, listed)
            start += size
    return jnp.where(listed > 0, 0.0, NEG_FILL)


def weigh(scores, bias, group, rate, before=None):
    peaks, weights = [], []
    for i in range(scores.shape[0] // group):
        piece = scores[i * group : (i + 1) * group] + bias[pl.ds(i, 1), :]
        peak = jnp.max(piece, axis=1, keepdims=True)
        if before is not None:
            peak = jnp.maximum(before[i], peak)
        peaks.append(peak)
        weights.append(jnp.exp2((piece - peak) * rate).astype(jnp.bfloat16))
    return peaks, jnp.concatenate(weights, axis=0)


def near_kernel(
    cols, pool_blocks, count, line, position, q_up, q_down, bound, passed, keys, values, pool_keys, pool_values, near,
    qs, sums, tops, norms, far_bias, ks, vs, tails, bias, sems,
):
    rows, width = qs.shape[0] // 2, qs.shape[1]
    group = rows // 2
    in_line = lax.rem(position[0], line)
    at_end = (in_line == 0, in_line == line - 1)
    near_keys, near_values = halves_of(near)
    blocks = [ref.at[pl.ds(i * group, group)] for ref in (q_up, q_down) for i in range(2)]
    copies = (
        fill(qs, blocks, sems, 0)
        + fill(ks, (keys, near_keys, pool_keys), sems, 4)
        + fill(vs, (values, near_values, pool_values), sems, 7)
    )
    for i in range(2):
        apart = fill(qs.at[pl.ds(i * rows, rows)], (bound.at[pl.ds(0, group)], passed), sems, 2 * i)
        corner = pl.ds(0, LANES)
        tail = tails.at[pl.ds(i * TILE, TILE)]
        source = (q_up, q_down)[i].at[pl.ds(rows, TILE), corner]
        copies.append(pltpu.make_async_copy(source, tail, sems.at[10 + i]))
        apart.append(pltpu.make_async_copy(bound.at[pl.ds(group, TILE), corner], tail, sems.at[10 + i]))

        @pl.when(at_end[i])
        def _():
            for copy in apart:
                copy.start()

        @pl.when(jnp.logical_not(at_end[i]))
        def _():
            for copy in (*copies[2 * i : 2 * i + 2], copies[10 + i]):
                copy.start()

    for copy in copies[4:10]:
        copy.start()
    for copy in copies:
        copy.wait()
    spot = Spot(position, cols, pool_blocks)
    for i in range(2):
        listed = numbers_of(tails[pl.ds(i * TILE, TILE), :], count)
        bias[pl.ds(2 * i, 2), :] = bias_of(listed, spot, ks.shape[0], True, group, pool_keys.shape[0])[:2]
        far_bias[pl.ds(2 * i, 2), :] = bias_of(listed, spot, LANES, False, group, pool_keys.shape[0])[:2]
    scale = 1.0 / math.sqrt(width // HEADS)
    ones = jnp.ones((ks.shape[0], LANES), jnp.bfloat16)
    for head in range(HEADS):
        part = pl.ds(head * LANES, LANES)
        scores = lax.dot_general(qs[:, part], ks[:, part], NT, preferred_element_type=jnp.float32)
        peaks, weights = weigh(scores, bias, group, scale * LOG2E)
        value = jnp.concatenate([vs[:, part], ones], axis=1)
        summed = jnp.dot(weights, value, preferred_element_type=jnp.float32)
        sums[:, part] = summed[:, :LANES]
        norms[:, part] = summed[:, LANES:]
        for i, peak in enumerate(peaks):
            tops[pl.ds(i * group, group), part] = jnp.broadcast_to(peak, (group, LANES))


def near_attention(shape, position, q_up, q_down, bound, passed, keys, values, pool_keys, pool_values, near):
    rows, width = keys.shape
    total = rows + near.shape[0] // 2 + pool_keys.shape[0]
    bf16, f32 = jnp.bfloat16, jnp.float32
    held, sent = pltpu.HBM, pl.ANY
    places = (pltpu.SMEM, sent, sent, sent, sent, held, held, held, held, sent)
    return pl.pallas_call(
        functools.partial(near_kernel, *shape),
        out_shape=[jax.ShapeDtypeStruct((2 * rows, width), kind) for kind in (bf16, f32, f32, f32)]
        + [jax.ShapeDtypeStruct((TILE, LANES), f32)],
        in_specs=[pl.BlockSpec(memory_space=place) for place in places],
        out_specs=[pl.BlockSpec(memory_space=pltpu.VMEM)] * 5,
        scratch_shapes=[
            pltpu.VMEM((total, width), bf16),
            pltpu.VMEM((total, width), bf16),
            pltpu.VMEM((2 * TILE, LANES), bf16),
            pltpu.VMEM((TILE, total), f32),
            pltpu.SemaphoreType.DMA((12,)),
        ],
        compiler_params=pltpu.CompilerParams(vmem_limit_bytes=11 << 20),
        cost_estimate=pl.CostEstimate(
            flops=4 * 2 * rows * total * width, bytes_accessed=4 << 20, transcendentals=2 * rows * total * HEADS
        ),
        name="near_attention",
    )(position, q_up, q_down, bound, passed, keys, values, pool_keys, pool_values, near)


def far_kernel(qs, sums, tops, norms, bias, far, out_up, out_down, ks, vs):
    edge = far.shape[0] // 2
    rows = out_up.shape[0]
    width = qs.shape[1]
    group = rows // 2
    scale = 1.0 / math.sqrt(width // HEADS)
    for part, scratch in ((0, ks), (1, vs)):
        scratch[pl.ds(0, edge), :] = far[pl.ds(part * edge, edge), :]
        scratch[pl.ds(edge, LANES - edge), :] = jnp.zeros((LANES - edge, width), scratch.dtype)
    lane = lax.broadcasted_iota(jnp.int32, (group, LANES), 1)
    zero = jnp.zeros((group, LANES), jnp.float32)
    kept_peak, kept_norm = [zero] * 4, [zero + 1.0] * 4
    ones = jnp.ones((LANES, LANES), jnp.bfloat16)
    outs = (out_up, out_down)
    spans = [pl.ds(i * group, group) for i in range(4)]
    for head in range(HEADS):
        part = pl.ds(head * LANES, LANES)
        scores = lax.dot_general(qs[:, part], ks[:, part], NT, preferred_element_type=jnp.float32)
        before = [tops[span, part] for span in spans]
        peaks, weights = weigh(scores, bias, group, scale * LOG2E, before)
        value = jnp.concatenate([vs[:, part], ones], axis=1)
        summed = jnp.dot(weights, value, preferred_element_type=jnp.float32)
        for i, span in enumerate(spans):
            factor = jnp.exp2((before[i] - peaks[i]) * (scale * LOG2E))
            piece = summed[i * group : (i + 1) * group]
            norm = norms[span, part] * factor + piece[:, LANES:]
            result = (sums[span, part] * factor + piece[:, :LANES]) / norm
            outs[i // 2][spans[i % 2], part] = result.astype(jnp.bfloat16)
            kept_peak[i] = jnp.where(lane == head, peaks[i], kept_peak[i])
            kept_norm[i] = jnp.where(lane == head, norm, kept_norm[i])
    for i in range(4):
        high, middle, low = split_in_three(kept_peak[i] * scale + jnp.log(kept_norm[i]))
        middle = pltpu.roll(middle.astype(jnp.float32), HEADS, 1)
        low = pltpu.roll(low.astype(jnp.float32), 2 * HEADS, 1)
        outs[i // 2][spans[i % 2], pl.ds(width, LANES)] = (high.astype(jnp.float32) + middle + low).astype(jnp.bfloat16)


def far_attention(qs, sums, tops, norms, bias, far):
    rows, width = qs.shape[0] // 2, qs.shape[1]
    message = jax.ShapeDtypeStruct((rows, width + LANES), jnp.bfloat16)
    return pl.pallas_call(
        far_kernel,
        out_shape=(message, message),
        in_specs=[pl.BlockSpec(memory_space=pltpu.VMEM)] * 6,
        out_specs=[pl.BlockSpec(memory_space=pltpu.VMEM)] * 2,
        scratch_shapes=[pltpu.VMEM((LANES, width), jnp.bfloat16)] * 2,
        compiler_params=pltpu.CompilerParams(vmem_limit_bytes=3 << 20),
        cost_estimate=pl.CostEstimate(
            flops=4 * 2 * rows * LANES * width, bytes_accessed=4 << 20, transcendentals=2 * rows * LANES * HEADS
        ),
        name="far_attention",
    )(qs, sums, tops, norms, bias, far)


def own_kernel(
    cols, pool_blocks, count, position, message, keys, values, pool_keys, pool_values, near, far, top_a, top_b,
    out, logs, qs, ks, vs, tail, bias, sems,
):
    rows, width = qs.shape
    group = rows // 2
    gap = ks.shape[0] - keys.shape[0] - near.shape[0] // 2 - pool_keys.shape[0] - far.shape[0] // 2 - 2 * top_a.shape[1]
    corner = message.at[pl.ds(rows, TILE), pl.ds(0, LANES)]
    copies = [
        pltpu.make_async_copy(message.at[pl.ds(0, rows)], qs, sems.at[0]),
        pltpu.make_async_copy(corner, tail, sems.at[13]),
    ]
    for part, scratch, mine, pool in ((0, ks, keys, pool_keys), (1, vs, values, pool_values)):
        spans = (top_a.at[part], top_b.at[part], mine, halves_of(near)[part], pool, halves_of(far)[part])
        copies += fill(scratch, spans, sems, 1 + 6 * part)
    for copy in copies:
        copy.start()
    for scratch in (ks, vs):
        scratch[pl.ds(ks.shape[0] - gap, gap), :] = jnp.zeros((gap, width), scratch.dtype)
    for copy in copies:
        copy.wait()
    spot = Spot(position, cols, pool_blocks)
    listed = numbers_of(tail[...], count)
    top, pool = 2 * top_a.shape[1], pool_keys.shape[0]
    chip = keys.shape[0] + near.shape[0] // 2 + pool
    bias[:, pl.ds(0, top)] = jnp.zeros((TILE, top), jnp.float32)
    bias[:, pl.ds(top, chip)] = bias_of(listed, spot, chip, True, group, pool)
    bias[:, pl.ds(top + chip, LANES)] = bias_of(listed, spot, LANES, False, group, pool)
    scale = 1.0 / math.sqrt(width // HEADS)
    ones = jnp.ones((ks.shape[0], LANES), jnp.bfloat16)
    for head in range(HEADS):
        part = pl.ds(head * LANES, LANES)
        scores = lax.dot_general(qs[:, part], ks[:, part], NT, preferred_element_type=jnp.float32)
        peaks, weights = weigh(scores, bias, group, scale * LOG2E)
        value = jnp.concatenate([vs[:, part], ones], axis=1)
        summed = jnp.dot(weights, value, preferred_element_type=jnp.float32)
        norm = summed[:, LANES:]
        out[:, part] = summed[:, :LANES] / norm
        for i, peak in enumerate(peaks):
            span = pl.ds(i * group, group)
            logs[span, part] = peak * scale + jnp.log(norm[i * group : (i + 1) * group])


def own_attention(shape, position, message, keys, values, pool_keys, pool_values, near, far, top_a, top_b):
    rows, width = keys.shape
    total = 2 * top_a.shape[1] + rows + near.shape[0] // 2 + pool_keys.shape[0] + LANES
    bf16, f32 = jnp.bfloat16, jnp.float32
    held, sent = pltpu.HBM, pl.ANY
    places = (pltpu.SMEM, sent, held, held, held, held, sent, sent, sent, sent)
    return pl.pallas_call(
        functools.partial(own_kernel, *shape),
        out_shape=[jax.ShapeDtypeStruct((rows, width), f32)] * 2,
        in_specs=[pl.BlockSpec(memory_space=place) for place in places],
        out_specs=[pl.BlockSpec(memory_space=pltpu.VMEM)] * 2,
        scratch_shapes=[
            pltpu.VMEM((rows, width), bf16),
            pltpu.VMEM((total, width), bf16),
            pltpu.VMEM((total, width), bf16),
            pltpu.VMEM((TILE, LANES), bf16),
            pltpu.VMEM((TILE, total), f32),
            pltpu.SemaphoreType.DMA((14,)),
        ],
        compiler_params=pltpu.CompilerParams(vmem_limit_bytes=8 << 20),
        cost_estimate=pl.CostEstimate(
            flops=4 * rows * total * width, bytes_accessed=4 << 20, transcendentals=rows * total * HEADS
        ),
        name="own_attention",
    )(position, message, keys, values, pool_keys, pool_values, near, far, top_a, top_b)


def merge_kernel(last, position, own, own_logs, above, below, out):
    _, width = out.shape
    tail = pl.ds(width, LANES)
    logs = []
    for i, ref in enumerate((above, below)):
        coded = ref[:, tail].astype(jnp.float32)
        log = coded + pltpu.roll(coded, LANES - HEADS, 1) + pltpu.roll(coded, LANES - 2 * HEADS, 1)
        logs.append(jnp.where(position[0] == last * i, NEG_FILL, log))
    for head in range(HEADS):
        part = pl.ds(head * LANES, LANES)
        own_log = own_logs[:, part]
        up_log, down_log = (jnp.broadcast_to(log[:, head : head + 1], own_log.shape) for log in logs)
        peak = jnp.maximum(jnp.maximum(own_log, up_log), down_log)
        shares = [jnp.exp(log - peak) for log in (own_log, up_log, down_log)]
        result = own[:, part] * shares[0]
        result = result + above[:, part].astype(jnp.float32) * shares[1]
        result = result + below[:, part].astype(jnp.float32) * shares[2]
        out[:, part] = (result / (shares[0] + shares[1] + shares[2])).astype(out.dtype)


def merge(rows_in_all, position, own, own_logs, above, below):
    return pl.pallas_call(
        functools.partial(merge_kernel, rows_in_all - 1),
        out_shape=jax.ShapeDtypeStruct(own.shape, jnp.bfloat16),
        in_specs=[pl.BlockSpec(memory_space=pltpu.SMEM)] + [pl.BlockSpec(memory_space=pltpu.VMEM)] * 4,
        out_specs=pl.BlockSpec(memory_space=pltpu.VMEM),
        compiler_params=pltpu.CompilerParams(vmem_limit_bytes=4 << 20),
        name="merge",
    )(position, own, own_logs, above, below)


def body(queries, keys, values, pool_keys, pool_values, top_keys, top_values, coarse_ids):
    _, _, blocks, tokens, width = queries.shape
    pool_blocks, pool_tokens, _ = pool_keys.shape
    rows = lax.axis_size("row")
    cols = lax.axis_size("col")
    row = lax.axis_index("row")
    col = lax.axis_index("col")
    position = jnp.stack([row, col]).astype(jnp.int32)
    pool = pool_blocks * pool_tokens
    own = blocks * tokens

    up = pairs(rows, cols, lambda r, q: (r - 1, q))
    down = pairs(rows, cols, lambda r, q: (r + 1, q))
    partner = pairs(rows, cols, lambda r, q: (r, q ^ 1))
    across = pairs(rows, cols, lambda r, q: (r, q + 1 if q % 2 else q - 1))
    line = rows // 4
    nowhere = (-1, -1)
    at_start = lambda r: r % line == 0
    at_end = lambda r: r % line == line - 1
    up_inside = pairs(rows, cols, lambda r, q: nowhere if at_start(r) else (r - 1, q))
    down_inside = pairs(rows, cols, lambda r, q: nowhere if at_end(r) else (r + 1, q))
    between = pairs(rows, cols, lambda r, q: (r + 1, q) if at_end(r) else (r - 1, q) if at_start(r) else nowhere)
    along_z = pairs(rows, cols, lambda r, q: (r + line, q) if at_end(r) else (r - line, q) if at_start(r) else nowhere)
    round_y = pairs(
        rows,
        cols,
        lambda r, q: (r - line + 1, q)
        if at_end(r) and r >= line
        else (r + line - 1, q)
        if at_start(r) and r < rows - line
        else nowhere,
    )
    halves = pairs(rows, cols, lambda r, q: ((3 - r // line) * line + r % line, q ^ 2))
    step_one = pairs(rows, cols, lambda r, q: (r, q ^ 4))
    step_two = pairs(rows, cols, lambda r, q: (r, q ^ 8))

    def stay(array, *shape):
        return pltpu.with_memory_space_constraint(array.reshape(shape), pltpu.HBM)

    pk = stay(pool_keys, pool, width)
    pv = stay(pool_values, pool, width)
    sources = (
        stay(queries, blocks, tokens, width),
        stay(keys, blocks, tokens, width),
        stay(values, blocks, tokens, width),
        pk,
        pv,
    )
    shares = (stay(top_keys, *top_keys.shape[1:]), stay(top_values, *top_values.shape[1:]))
    ids = coarse_ids.reshape(blocks, -1)
    edge = (2 * (tokens + pool), width)
    far, second = packed(pack_far_kernel, [edge, (tokens, width)], [position], sources, 5)
    passed = send(second, along_z)
    far = send(far, across)
    near, top, message, bound = packed(
        pack_near_kernel,
        [edge, (2,) + top_keys.shape[1:], (own + TILE, width), (tokens + TILE, width)],
        [position, ids],
        sources + shares,
        9,
    )
    bound = send(bound, between)
    q_down = send(message, up_inside)
    q_up = send(message, down_inside)
    near = send(near, partner)
    passed = send(passed, round_y)
    for links in (step_one, step_two, halves):
        top = join(top, send(top, links))
    top_other = send(top, partner)

    shape = (cols, pool_blocks, ids.shape[1])
    kept_keys, kept_values = stay(keys, own, width), stay(values, own, width)
    near_parts = near_attention(
        shape + (line,), position, q_up, q_down, bound, passed, kept_keys, kept_values, pk, pv, near
    )
    to_up, to_down = far_attention(*near_parts, far)
    below = send(to_up, up)
    above = send(to_down, down)
    mine = own_attention(shape, position, message, kept_keys, kept_values, pk, pv, near, far, top, top_other)
    return merge(rows, position, *mine, above, below).reshape(queries.shape)


def solution(mesh):
    placed = (
        P(None, "row", "col", None, None),
        P(None, "row", "col", None, None),
        P(None, "row", "col", None, None),
        P(("row", "col"), None, None),
        P(("row", "col"), None, None),
        P(None, "col", None),
        P(None, "col", None),
        P(None, "row", "col", None),
    )

    return jax.shard_map(
        body,
        mesh=mesh,
        in_specs=placed,
        out_specs=P(None, "row", "col", None, None),
        check_vma=False,
    )
```
